128 devices in a mesh: ctx: 32 (over y, z, core), grp: 4 (over x).
Axes of the slice: x: 4, y: 4, z: 4, core: 2. Of those that a mesh axis runs over, the one named last changes fastest.
Arguments:
- queries: bfloat16 [131072, 1024], P(('grp', 'ctx')), parts along dimension 0, may hold values from -130 to 130
- keys: bfloat16 [131072, 128], P(('grp', 'ctx')), parts along dimension 0, may hold values from -4 to 4
- values: bfloat16 [131072, 128], P(('grp', 'ctx')), parts along dimension 0, may hold values from -6 to 6
- dout: bfloat16 [131072, 1024], P(('grp', 'ctx')), parts along dimension 0, may hold values from -6 to 6
- glob_keys: bfloat16 [2048, 128], P('grp'), parts along dimension 0, may hold values from -6 to 6
- glob_values: bfloat16 [2048, 128], P('grp'), parts along dimension 0, may hold values from -6 to 6
- frames: int32 [131072], P(('grp', 'ctx')), parts along dimension 0, may hold values from 0 to 255, never falling along the last dimension, each value on 1 to 256 neighbouring positions
- far_owner: int32 [2048, 2], P('grp'), parts along dimension 0, may hold values from 0 to 31, all different within a row; in each aligned block of 16 rows (0 to 15, 16 to 31, ...) at most 2 rows name the same one
- far_local: int32 [2048, 2], P('grp'), parts along dimension 0, may hold values from 0 to 15
Outputs:
- query_grad: float32 [131072, 1024], P(('grp', 'ctx')), parts along dimension 0
- key_grad: float32 [131072, 128], P(('grp', 'ctx')), parts along dimension 0
- value_grad: float32 [131072, 128], P(('grp', 'ctx')), parts along dimension 0
- glob_key_grad: float32 [2048, 128], P('grp'), parts along dimension 0
- glob_value_grad: float32 [2048, 128], P('grp'), parts along dimension 0
The draws below stay inside these ranges and needn't reach their ends.
There are 4 independent parts, one for each index of `grp`. The reference program is written for one: setup_inputs(seed, part) draws one part's arguments, and reference() takes and returns one part's arrays. A program takes and returns all parts, laid end to end along the dimension named above; each array names one. Nothing has to cross between parts.
Inputs may be any that keep to these rules, and one draw needn't show every extreme that they name: `far_owner`: among the 16 query blocks of one index of ctx, no ctx index is named as owner by more than 2 of them; the 2 owners of one query block differ. `frames`: frame numbers never fall along the sequence.
All inputs are finite; a program needn't handle non-finite values.
Results may differ from the reference program's by a relative error of at most 0.02.
The reference program's roundings to bfloat16 on the way count: a program that leaves them out, or rounds other values in their place, can miss the bound.
Values may be sent and summed in bfloat16 or wider, within the bound.
A program may use at most 128 MiB of HBM per device.

```python
import math
import jax
import jax.numpy as jnp
import numpy as np
from jax import lax

HEADS = 8
HEAD_DIM = 128
BLOCK = 64
GLOBALS = 512
FAR = 2
TOKENS = 32768
BLOCKS_DEV = 16
QBLOCKS = 512
SLOTS = 2
FRAMES = 256
N_CTX = 32


def paired_fields(key):
    key_rows = jnp.clip(jax.random.normal(jax.random.fold_in(key, 7), (TOKENS, HEAD_DIM), jnp.float32), -4.0, 4.0)
    query_rows = jnp.clip(jax.random.normal(jax.random.fold_in(key, 8), (TOKENS, HEADS * HEAD_DIM), jnp.float32), -4.0, 4.0)
    return (query_rows, key_rows)


def draw_queries(key, part):
    return paired_fields(key)[0].astype(jnp.bfloat16)


def draw_keys(key, part):
    return paired_fields(key)[1].astype(jnp.bfloat16)


def plant(array, stream_key, smallest, top_value):
    place = [jax.random.randint(jax.random.fold_in(stream_key, axis), (), 0, length) for axis, length in enumerate(array.shape)]
    longest = array.shape.index(max(array.shape))
    neighbour = place[:longest] + [(place[longest] + 1) % array.shape[longest]] + place[longest + 1:]
    return array.at[tuple(place)].set(smallest).at[tuple(neighbour)].set(top_value)


def block_scale(own_key, extent, split, low, largest):
    loudness = 1.0
    for axis_at, shards_of in split:
        draws = jax.random.uniform(jax.random.fold_in(jax.random.fold_in(own_key, 6), axis_at), (shards_of,), jnp.float32, low / len(split), largest / len(split))
        loudness = loudness * jnp.repeat(jnp.exp(draws), extent[axis_at] // shards_of).reshape((-1,) + (1,) * (len(extent) - 1 - axis_at))
    return loudness


def length_profile(amount, total, most, slope):
    weights = [(1 << 20) // math.isqrt(grade ** slope) + 1 for grade in range(2, amount + 1)]
    rest, holding = total - most - (amount - 1), [1] * (amount - 1)
    while rest > 0:
        candidates = [i for i in range(amount - 1) if holding[i] < most]
        mass, left = sum([weights[i] for i in candidates]), rest
        for i in candidates:
            more = min(most - holding[i], max(1, left * weights[i] // mass), rest)
            holding[i] = holding[i] + more
            rest = rest - more
    return np.array([most] + holding)


def ragged_sizes(key, count, total, bound, slope):
    if count == 2:
        one = jax.random.randint(key, (), max(1, total - bound), min(bound, total - 1) + 1)
        return jnp.stack([one, total - one])
    tallies = jnp.asarray(length_profile(count, total, bound, slope), jnp.int32)
    pairs = (count - 1) // 2
    donor, sink = tallies[1:1 + 2 * pairs:2], tallies[2:2 + 2 * pairs:2]
    room = jnp.minimum(donor - 1, bound - sink)
    shifted = jax.random.randint(jax.random.fold_in(key, 1), (pairs,), 0, 1 << 20) % (room + 1)
    tallies = tallies.at[1:1 + 2 * pairs:2].set(donor - shifted).at[2:2 + 2 * pairs:2].set(sink + shifted)
    return tallies[jax.random.permutation(jax.random.fold_in(key, 2), count)]


def deal_out(rng, own, number, rows, count, top, most, slope):
    sequence = jax.random.permutation(rng, count)
    heavy_load, usual = portions_of(count, rows * top, most, slope, True), portions_of(count, rows * top, most, slope, False)
    places = jnp.arange(count)

    def named(tallies, offset_by):
        used = int((tallies > 0).sum())
        fixed = max(1, used // 4)
        passed = fixed + (places - fixed + offset_by * (used - fixed)) % max(1, count - fixed)
        return jnp.zeros((count,), jnp.int32).at[sequence[jnp.where(places < fixed, places, passed)]].set(jnp.asarray(tallies, jnp.int32))

    tallies = jnp.where(number % 4 == 0, named(heavy_load, number // 4), named(usual, number - number // 4 - 1))
    mixed = jax.random.permutation(jax.random.fold_in(own, 3), count)
    donor, sink = mixed[0:count // 2 * 2:2], mixed[1:count // 2 * 2:2]
    slack = jnp.minimum(tallies[donor] - 1, most - tallies[sink]) // 2
    slack = jnp.where((donor == sequence[0]) | (sink == sequence[0]) | (tallies[sink] == 0), 0, jnp.maximum(slack, 0))
    passed = jax.random.randint(jax.random.fold_in(own, 4), (count // 2,), 0, 1 << 20) % (slack + 1)
    tallies = tallies.at[donor].add(-passed).at[sink].add(passed)
    items = jnp.searchsorted(jnp.cumsum(tallies), jnp.arange(rows * top), side="right").astype(jnp.int32)
    table = items.reshape(top, rows).T
    table = table[jax.random.permutation(jax.random.fold_in(own, 1), rows)]
    offset_by = jax.random.randint(jax.random.fold_in(own, 2), (rows, 1), 0, top)
    return jnp.take_along_axis(table, (jnp.arange(top)[None, :] + offset_by) % top, axis=1)


def portions_of(amount, total, most, slope, full):
    portions = [(1 << 20) // math.isqrt(rank ** slope) + 1 for rank in range(1, amount + 1)]
    largest = most if full else min(most, max(-(-total // amount), total * portions[0] // sum(portions)))
    least = 1 if total - largest >= amount - 1 else 0
    given, spare = [largest] + [least] * (amount - 1), total - largest - least * (amount - 1)
    while spare > 0:
        candidates = [i for i in range(1, amount) if given[i] < largest] or [i for i in range(1, amount) if given[i] < most]
        mass, left = sum([portions[i] for i in candidates]), spare
        for i in candidates:
            more = min(most - given[i], max(1, left * portions[i] // mass), spare)
            given[i] = given[i] + more
            spare = spare - more
    return np.array(given)


def scatter_about(rng, dims, spread, reach, pieces=(), kind=jnp.bfloat16):
    array = jax.random.normal(rng, dims, jnp.float32) * spread
    if len(pieces) > 0:
        array = block_scale(rng, dims, pieces, -0.22, 0.18) * array
    return jnp.clip(array, min=-reach, max=reach).astype(kind)


def setup_inputs(seed: int = 0, part: int = 0) -> dict:
    seeds = jax.random.split(jax.random.key(seed), 10)
    part_keys = jax.random.split(jax.random.fold_in(seeds[9], part), 10)
    queries = draw_queries(jax.random.fold_in(jax.random.fold_in(seeds[9], part), 71), part)
    keys = draw_keys(jax.random.fold_in(jax.random.fold_in(seeds[9], part), 71), part)
    values = scatter_about(part_keys[2], (TOKENS, HEAD_DIM), 1.0, 6.0, ((0, 32),))
    dout = scatter_about(part_keys[3], (TOKENS, HEADS * HEAD_DIM), 1.0, 6.0, ((0, 32),))
    glob_keys = scatter_about(part_keys[4], (GLOBALS, HEAD_DIM), 1.0, 6.0)
    glob_values = scatter_about(part_keys[5], (GLOBALS, HEAD_DIM), 1.0, 6.0)
    frames = jnp.searchsorted(jnp.cumsum(ragged_sizes(part_keys[6], FRAMES, TOKENS, 256, 1)), jnp.arange(TOKENS), side="right").astype(jnp.int32)
    far_owner_keys = jax.random.split(jax.random.fold_in(part_keys[7], 1), QBLOCKS // BLOCKS_DEV)
    far_owner_turns = jax.random.permutation(jax.random.fold_in(part_keys[7], 3), QBLOCKS // BLOCKS_DEV)
    far_owner = jax.vmap(lambda own, number: deal_out(jax.random.fold_in(part_keys[7], 2), own, number, BLOCKS_DEV, N_CTX, FAR, SLOTS, 2))(far_owner_keys, far_owner_turns).reshape((QBLOCKS, FAR))
    far_local = plant(jax.random.randint(part_keys[8], (QBLOCKS, FAR), 0, BLOCKS_DEV), jax.random.fold_in(part_keys[8], 1), 0, BLOCKS_DEV - 1).astype(jnp.int32)
    return dict(queries=queries, keys=keys, values=values, dout=dout, glob_keys=glob_keys, glob_values=glob_values, frames=frames, far_owner=far_owner, far_local=far_local)


rope_base = 1000000.0
yarn_factor = 4.0
orig_context = 32768.0
ramp_low = 1.0
ramp_high = 32.0

def rotary_tables(frame_ids, head_width):
    half_width = head_width // 2
    pair_index = jnp.arange(half_width).astype(jnp.float32)
    inverse = rope_base ** (-2.0 * pair_index / head_width)
    ratios = orig_context * inverse / (2.0 * math.pi)
    ramp_mix = jnp.clip((ratios - ramp_low) / (ramp_high - ramp_low), 0.0, 1.0)
    frequency = inverse * ((1.0 - ramp_mix) / yarn_factor + ramp_mix)
    angles = frame_ids.astype(jnp.float32)[:, None] * frequency[None, :]
    return (jnp.cos(angles), jnp.sin(angles))

def rotate(field, cosine, sine_table):
    half_width = field.shape[-1] // 2
    first_half = field[..., :half_width]
    second_half = field[..., half_width:]
    cos_rows = cosine[:, None, :]
    sin_rows = sine_table[:, None, :]
    return jnp.concatenate([first_half * cos_rows - second_half * sin_rows, second_half * cos_rows + first_half * sin_rows], axis=-1)

def score_factor(head_width):
    return (0.1 * math.log(yarn_factor) + 1.0) ** 2 / math.sqrt(head_width)

def block_grads(query_rows, grad_rows, keyset, valset, factor):
    scores = lax.dot_general(query_rows, keyset, (((1,), (1,)), ((), ())), preferred_element_type=jnp.float32) * factor
    row_max = lax.optimization_barrier(jnp.max(scores, axis=-1, keepdims=True))
    exp_scores = jnp.exp(scores - row_max)
    prob_full = exp_scores / lax.optimization_barrier(jnp.sum(exp_scores, axis=-1, keepdims=True))
    prob_low = prob_full.astype(jnp.bfloat16)
    dprob = lax.dot_general(grad_rows, valset, (((1,), (1,)), ((), ())), preferred_element_type=jnp.float32)
    row_delta = lax.optimization_barrier(jnp.sum(prob_full * dprob, axis=-1, keepdims=True))
    dscore = (prob_full * (dprob - row_delta)).astype(jnp.bfloat16)
    q_grad = jnp.dot(dscore, keyset, preferred_element_type=jnp.float32) * factor
    k_grad = lax.dot_general(dscore, query_rows, (((0,), (0,)), ((), ())), preferred_element_type=jnp.float32) * factor
    v_grad = lax.dot_general(prob_low, grad_rows, (((0,), (0,)), ((), ())), preferred_element_type=jnp.float32)
    return (q_grad, k_grad, v_grad)

def reference(queries, keys, values, dout, glob_keys, glob_values, frames, far_owner, far_local):
    factor = score_factor(HEAD_DIM)
    cosine, sine_table = rotary_tables(frames, HEAD_DIM)
    qrot = rotate(queries.astype(jnp.float32).reshape(TOKENS, HEADS, HEAD_DIM), cosine, sine_table).astype(jnp.bfloat16)
    krot = rotate(keys.astype(jnp.float32)[:, None, :], cosine, sine_table)[:, 0].astype(jnp.bfloat16)
    query_blocks = qrot.reshape(QBLOCKS, BLOCK * HEADS, HEAD_DIM)
    grad_blocks = dout.reshape(QBLOCKS, BLOCK * HEADS, HEAD_DIM)
    key_blocks = krot.reshape(QBLOCKS, BLOCK, HEAD_DIM)
    value_blocks = values.reshape(QBLOCKS, BLOCK, HEAD_DIM)
    far_block = (far_owner * BLOCKS_DEV + far_local).astype(jnp.int32)

    def advance(running, block_index):
        key_total, value_total, glob_k, glob_v = running
        far_ids = far_block[block_index]
        keyset = jnp.concatenate([glob_keys, key_blocks[block_index], key_blocks[far_ids].reshape(FAR * BLOCK, HEAD_DIM)], axis=0)
        valset = jnp.concatenate([glob_values, value_blocks[block_index], value_blocks[far_ids].reshape(FAR * BLOCK, HEAD_DIM)], axis=0)
        q_grad, k_grad, v_grad = block_grads(query_blocks[block_index], grad_blocks[block_index], keyset, valset, factor)
        glob_k = glob_k + k_grad[:GLOBALS]
        glob_v = glob_v + v_grad[:GLOBALS]
        key_total = key_total.at[block_index].add(k_grad[GLOBALS:GLOBALS + BLOCK])
        value_total = value_total.at[block_index].add(v_grad[GLOBALS:GLOBALS + BLOCK])
        key_total = key_total.at[far_ids].add(k_grad[GLOBALS + BLOCK:].reshape(FAR, BLOCK, HEAD_DIM))
        value_total = value_total.at[far_ids].add(v_grad[GLOBALS + BLOCK:].reshape(FAR, BLOCK, HEAD_DIM))
        return ((key_total, value_total, glob_k, glob_v), q_grad)
    start_state = (jnp.zeros((QBLOCKS, BLOCK, HEAD_DIM), jnp.float32), jnp.zeros((QBLOCKS, BLOCK, HEAD_DIM), jnp.float32), jnp.zeros((GLOBALS, HEAD_DIM), jnp.float32), jnp.zeros((GLOBALS, HEAD_DIM), jnp.float32))
    final_state, q_grads = lax.scan(advance, start_state, jnp.arange(QBLOCKS).astype(jnp.int32))
    key_total, value_total, glob_k, glob_v = final_state
    query_grad = rotate(q_grads.reshape(TOKENS, HEADS, HEAD_DIM), cosine, -sine_table).reshape(TOKENS, HEADS * HEAD_DIM)
    key_grad = rotate(key_total.reshape(TOKENS, 1, HEAD_DIM), cosine, -sine_table)[:, 0]
    return (query_grad, key_grad, value_total.reshape(TOKENS, HEAD_DIM), glob_k, glob_v)
```

```python
import functools
import math

import jax
import jax.numpy as jnp
from jax import lax
from jax.experimental import pallas as pl
from jax.experimental.pallas import tpu as pltpu
from jax.sharding import PartitionSpec as P

F32, BF16 = jnp.float32, jnp.bfloat16
MESH = pl.DeviceIdType.MESH
BLOCK, FAR, SLOTS, D, HEADS = 64, 2, 2, 128, 8
ROWS = BLOCK * HEADS

rope_base = 1000000.0
yarn_factor = 4.0
orig_context = 32768.0
ramp_low = 1.0
ramp_high = 32.0

FACTOR = (0.1 * math.log(yarn_factor) + 1.0) ** 2 / math.sqrt(D)
FACTOR2 = FACTOR * math.log2(math.e)

NT = (((1,), (1,)), ((), ()))
NN = (((1,), (0,)), ((), ()))


def dot(a, b, dims):
    return lax.dot_general(a, b, dims, preferred_element_type=F32)


def rotary_tables(frame_ids):
    half = D // 2
    index = jnp.arange(half).astype(F32)
    inverse = rope_base ** (-2.0 * index / D)
    ratios = orig_context * inverse / (2.0 * math.pi)
    ramp = jnp.clip((ratios - ramp_low) / (ramp_high - ramp_low), 0.0, 1.0)
    frequency = inverse * ((1.0 - ramp) / yarn_factor + ramp)
    angles = frame_ids.astype(F32)[:, None] * frequency[None, :]
    cosine, sine = jnp.cos(angles), jnp.sin(angles)
    return (
        jnp.concatenate([cosine, cosine], axis=1),
        jnp.concatenate([-sine, sine], axis=1),
    )


def rot(x, c, s):
    return x * c + pltpu.roll(x, D // 2, 1) * s


def unrot(x, c, s):
    return x * c - pltpu.roll(x, D // 2, 1) * s


def prep_kernel(local_ref, k_ref, v_ref, c_ref, s_ref, own_ref, send_ref):
    blocks = own_ref.shape[0]
    for b in range(blocks):
        rows = slice(b * BLOCK, (b + 1) * BLOCK)
        own_ref[b, :, :D] = rot(k_ref[rows].astype(F32), c_ref[rows], s_ref[rows]).astype(BF16)
        own_ref[b, :, D:] = v_ref[rows]

    def put(i, carry):
        for j in range(SLOTS):
            send_ref[i, j * BLOCK : (j + 1) * BLOCK] = own_ref[local_ref[i * SLOTS + j]]
        return carry

    lax.fori_loop(0, send_ref.shape[0], put, 0)


def prep(local, keys, values, c, s, n):
    blocks = keys.shape[0] // BLOCK
    return pl.pallas_call(
        prep_kernel,
        in_specs=[pl.BlockSpec(memory_space=pltpu.SMEM)]
        + [pl.BlockSpec(memory_space=pltpu.VMEM)] * 4,
        out_specs=[pl.BlockSpec(memory_space=pltpu.VMEM)] * 2,
        out_shape=[
            jax.ShapeDtypeStruct((blocks, BLOCK, 2 * D), BF16),
            jax.ShapeDtypeStruct((n, SLOTS * BLOCK, 2 * D), BF16),
        ],
        compiler_params=pltpu.CompilerParams(vmem_limit_bytes=32 << 20),
        name="prep",
    )(local, keys, values, c, s)


def attn_kernel(
    shard, slot_ref, q_ref, do_ref, c_ref, s_ref, own_ref, recv_ref, gk_ref, gv_ref,
    dq_ref, dkv_ref, ret_ref, kset, vset, kt, qr, dor, pb, dsb, gacc,
):
    b = pl.program_id(0)
    g = gk_ref.shape[0]

    @pl.when(b == 0)
    def _():
        kset[:g] = gk_ref[...]
        vset[:g] = gv_ref[...]
        kt[:, :g] = gk_ref[...].T
        gacc[...] = jnp.zeros_like(gacc)

    own = own_ref[0]
    places = []
    for f in range(FAR):
        slot = slot_ref[b * FAR + f]
        places.append((slot // SLOTS, pl.ds(pl.multiple_of((slot % SLOTS) * BLOCK, BLOCK), BLOCK)))
    parts = [own] + [recv_ref[o, r, :] for o, r in places]
    kk = jnp.concatenate([x[:, :D] for x in parts], axis=0)
    kset[g:] = kk
    vset[g:] = jnp.concatenate([x[:, D:] for x in parts], axis=0)
    kt[:, g:] = kk.T
    c, s = c_ref[...], s_ref[...]
    for h in range(HEADS):
        at, cols = slice(h * BLOCK, (h + 1) * BLOCK), slice(h * D, (h + 1) * D)
        qr[at] = rot(q_ref[:, cols].astype(F32), c, s).astype(BF16)
        dor[at] = do_ref[:, cols]
    width = 256
    for j in range(0, ROWS, width):
        at = slice(j, j + width)
        scores = dot(kset[...], qr[at], NT)
        dp = dot(vset[...], dor[at], NT)
        top = jnp.max(scores, axis=0, keepdims=True)
        e = jnp.exp2(scores * FACTOR2 - top * FACTOR2)
        total = jnp.sum(e, axis=0, keepdims=True)
        mixed = jnp.sum(e * dp, axis=0, keepdims=True)
        w = 1.0 / total
        delta = mixed * w
        p = e * w
        pb[:, at] = p.astype(BF16)
        dsb[:, at] = (p * (dp - delta)).astype(BF16)
    dq = dot(kt[...], dsb[...], NN).T
    dk = dot(dsb[...], qr[...], NN) * FACTOR
    dv = dot(pb[...], dor[...], NN)
    for h in range(HEADS):
        y = dq[h * BLOCK : (h + 1) * BLOCK] * FACTOR
        dq_ref[:, h * D : (h + 1) * D] = unrot(y, c, s)
    gacc[:, :D] += dk[:g]
    gacc[:, D:] += dv[:g]
    dkv_ref[:, :D] = dk[g : g + BLOCK]
    dkv_ref[:, D:] = dv[g : g + BLOCK]
    for f, (o, r) in enumerate(places):
        at = slice(g + BLOCK * (1 + f), g + BLOCK * (2 + f))
        ret_ref[o, r, :] = jnp.concatenate([dk[at], dv[at]], axis=1).astype(BF16)

    @pl.when(b == pl.num_programs(0) - 1)
    def _():
        for i in range(ret_ref.shape[0]):
            ret_ref[i, SLOTS * BLOCK :, :] = gacc[i * shard : (i + 1) * shard].astype(BF16)


def attn(slots, q, do, c, s, own, recv, gk, gv):
    n, g = recv.shape[0], gk.shape[0]
    shard = g // n
    blocks = own.shape[0]
    keyrows = g + BLOCK * (1 + FAR)
    tile = lambda b, t: (b, 0)
    whole2 = lambda b, t: (0, 0)
    whole3 = lambda b, t: (0, 0, 0)
    tok = q.shape[0]
    retrows = SLOTS * BLOCK + shard
    return pl.pallas_call(
        functools.partial(attn_kernel, shard),
        grid_spec=pltpu.PrefetchScalarGridSpec(
            num_scalar_prefetch=1,
            grid=(blocks,),
            in_specs=[
                pl.BlockSpec((BLOCK, HEADS * D), tile),
                pl.BlockSpec((BLOCK, HEADS * D), tile),
                pl.BlockSpec((BLOCK, D), tile),
                pl.BlockSpec((BLOCK, D), tile),
                pl.BlockSpec((1, BLOCK, 2 * D), lambda b, t: (b, 0, 0)),
                pl.BlockSpec((n, SLOTS * BLOCK, 2 * D), whole3),
                pl.BlockSpec((g, D), whole2),
                pl.BlockSpec((g, D), whole2),
            ],
            out_specs=[
                pl.BlockSpec((BLOCK, HEADS * D), tile),
                pl.BlockSpec((BLOCK, 2 * D), tile),
                pl.BlockSpec((n, retrows, 2 * D), whole3),
            ],
            scratch_shapes=[
                pltpu.VMEM((keyrows, D), BF16),
                pltpu.VMEM((keyrows, D), BF16),
                pltpu.VMEM((D, keyrows), BF16),
                pltpu.VMEM((ROWS, D), BF16),
                pltpu.VMEM((ROWS, D), BF16),
                pltpu.VMEM((keyrows, ROWS), BF16),
                pltpu.VMEM((keyrows, ROWS), BF16),
                pltpu.VMEM((g, 2 * D), F32),
            ],
        ),
        out_shape=[
            jax.ShapeDtypeStruct((tok, HEADS * D), F32),
            jax.ShapeDtypeStruct((tok, 2 * D), F32),
            jax.ShapeDtypeStruct((n, retrows, 2 * D), BF16),
        ],
        compiler_params=pltpu.CompilerParams(vmem_limit_bytes=48 << 20),
        name="attn",
    )(slots, q, do, c, s, own, recv, gk, gv)


def final_kernel(local_ref, valid_ref, dkv_ref, back_ref, c_ref, s_ref, kg_ref, vg_ref, gs_ref, acc):
    n = back_ref.shape[0]
    blocks = acc.shape[0]
    for b in range(blocks):
        acc[b] = dkv_ref[b * BLOCK : (b + 1) * BLOCK]

    def add(i, carry):
        for j in range(SLOTS):

            @pl.when(valid_ref[i * SLOTS + j] > 0)
            def _():
                at = local_ref[i * SLOTS + j]
                acc[at] += back_ref[i, j * BLOCK : (j + 1) * BLOCK].astype(F32)

        return carry

    lax.fori_loop(0, n, add, 0)
    for b in range(blocks):
        rows = slice(b * BLOCK, (b + 1) * BLOCK)
        kg_ref[rows] = unrot(acc[b, :, :D], c_ref[rows], s_ref[rows])
        vg_ref[rows] = acc[b, :, D:]
    gs_ref[...] = jnp.sum(back_ref[:, SLOTS * BLOCK :, :].astype(F32), axis=0).astype(BF16)


def final(local, valid, dkv, back, c, s):
    n, retrows, _ = back.shape
    shard = retrows - SLOTS * BLOCK
    tok = dkv.shape[0]
    return pl.pallas_call(
        final_kernel,
        in_specs=[pl.BlockSpec(memory_space=pltpu.SMEM)] * 2
        + [pl.BlockSpec(memory_space=pltpu.VMEM)] * 4,
        out_specs=[pl.BlockSpec(memory_space=pltpu.VMEM)] * 3,
        out_shape=[
            jax.ShapeDtypeStruct((tok, D), F32),
            jax.ShapeDtypeStruct((tok, D), F32),
            jax.ShapeDtypeStruct((shard, 2 * D), BF16),
        ],
        scratch_shapes=[pltpu.VMEM((tok // BLOCK, BLOCK, 2 * D), F32)],
        compiler_params=pltpu.CompilerParams(vmem_limit_bytes=32 << 20),
        name="final",
    )(local, valid, dkv, back, c, s)


def spread_kernel(n, x_ref, k_ref, v_ref, held, ssem, rsem):
    me = lax.axis_index("ctx")
    barrier = pltpu.get_barrier_semaphore()

    def greet(r, carry):
        pl.semaphore_signal(
            barrier, inc=1, device_id={"ctx": lax.rem(me + r, n)}, device_id_type=MESH
        )
        return carry

    lax.fori_loop(1, n, greet, 0)
    pl.semaphore_wait(barrier, n - 1)

    def copy(r):
        return pltpu.make_async_remote_copy(
            x_ref, held.at[me], ssem.at[r], rsem.at[r],
            device_id={"ctx": lax.rem(me + r, n)}, device_id_type=MESH,
        )

    def start(r, carry):
        copy(r).start()
        return carry

    lax.fori_loop(1, n, start, 0)
    held[me] = x_ref[...]

    def finish(r, carry):
        copy(r).wait()
        return carry

    lax.fori_loop(1, n, finish, 0)
    shard = x_ref.shape[0]
    for i in range(n):
        k_ref[i * shard : (i + 1) * shard] = held[i, :, :D].astype(F32)
        v_ref[i * shard : (i + 1) * shard] = held[i, :, D:].astype(F32)


def spread(x, n):
    shard = x.shape[0]
    return pl.pallas_call(
        functools.partial(spread_kernel, n),
        in_specs=[pl.BlockSpec(memory_space=pltpu.VMEM)],
        out_specs=[pl.BlockSpec(memory_space=pltpu.VMEM)] * 2,
        out_shape=[jax.ShapeDtypeStruct((n * shard, D), F32)] * 2,
        scratch_shapes=[
            pltpu.VMEM((n, shard, 2 * D), BF16),
            pltpu.SemaphoreType.DMA((n,)),
            pltpu.SemaphoreType.DMA((n,)),
        ],
        compiler_params=pltpu.CompilerParams(collective_id=0, has_side_effects=True),
        name="spread",
    )(x)


def on_device(queries, keys, values, dout, glob_keys, glob_values, frames, far_owner, far_local):
    n = lax.axis_size("ctx")
    me = lax.axis_index("ctx")
    blocks = keys.shape[0] // BLOCK
    entries = blocks * FAR
    c, s = rotary_tables(frames)
    owners = far_owner.reshape(n, entries)
    locals_ = far_local.reshape(n, entries)
    place = jnp.arange(entries)
    rank = jnp.sum(
        (owners[:, :, None] == owners[:, None, :]) & (place[None, :] < place[:, None]), axis=-1
    )
    slots = lax.dynamic_index_in_dim(owners * SLOTS + rank, me, 0, keepdims=False)
    chosen = (owners == me)[:, None, :] & (rank[:, None, :] == jnp.arange(SLOTS)[None, :, None])
    local = jnp.sum(jnp.where(chosen, locals_[:, None, :], 0), axis=-1).reshape(-1)
    valid = jnp.sum(chosen.astype(jnp.int32), axis=-1).reshape(-1)

    own, send = prep(local, keys, values, c, s, n)
    recv = lax.all_to_all(send, "ctx", split_axis=0, concat_axis=0, tiled=True)
    dq, dkv, ret = attn(slots, queries, dout, c, s, own, recv, glob_keys, glob_values)
    back = lax.all_to_all(ret, "ctx", split_axis=0, concat_axis=0, tiled=True)
    kg, vg, gs = final(local, valid, dkv, back, c, s)
    gk, gv = spread(gs, n)
    return dq, kg, vg, gk, gv


def solution(mesh):
    both = P(("grp", "ctx"), None)
    one = P("grp", None)
    return jax.shard_map(
        on_device,
        mesh=mesh,
        in_specs=(both, both, both, both, one, one, P(("grp", "ctx")), one, one),
        out_specs=(both, both, both, one, one),
        check_vma=False,
    )
```

```python
import functools
import math

import jax
import jax.numpy as jnp
from jax import lax
from jax.experimental import pallas as pl
from jax.experimental.pallas import tpu as pltpu
from jax.sharding import PartitionSpec as P

F32, BF16 = jnp.float32, jnp.bfloat16
MESH = pl.DeviceIdType.MESH
BLOCK, FAR, SLOTS, D, HEADS = 64, 2, 2, 128, 8
ROWS = BLOCK * HEADS

rope_base = 1000000.0
yarn_factor = 4.0
orig_context = 32768.0
ramp_low = 1.0
ramp_high = 32.0

FACTOR = (0.1 * math.log(yarn_factor) + 1.0) ** 2 / math.sqrt(D)
FACTOR2 = FACTOR * math.log2(math.e)

NT = (((1,), (1,)), ((), ()))
NN = (((1,), (0,)), ((), ()))
TN = (((0,), (0,)), ((), ()))


def dot(a, b, dims):
    return lax.dot_general(a, b, dims, preferred_element_type=F32)


def rotary_tables(frame_ids):
    half = D // 2
    index = jnp.arange(half).astype(F32)
    inverse = rope_base ** (-2.0 * index / D)
    ratios = orig_context * inverse / (2.0 * math.pi)
    ramp = jnp.clip((ratios - ramp_low) / (ramp_high - ramp_low), 0.0, 1.0)
    frequency = inverse * ((1.0 - ramp) / yarn_factor + ramp)
    angles = frame_ids.astype(F32)[:, None] * frequency[None, :]
    cosine, sine = jnp.cos(angles), jnp.sin(angles)
    return (
        jnp.concatenate([cosine, cosine], axis=1),
        jnp.concatenate([-sine, sine], axis=1),
    )


def rot(x, c, s):
    return x * c + pltpu.roll(x, D // 2, 1) * s


def unrot(x, c, s):
    return x * c - pltpu.roll(x, D // 2, 1) * s


def send_plan(i, n):
    return 1 + lax.rem(i * 11, n - 1)


def main_kernel(
    n, local_ref, slot_ref, entry_ref, k_ref, v_ref, c_ref, s_ref, gk_ref, gv_ref, q_hbm, do_hbm,
    dq_hbm, dkv_ref, back_ref, glob_ref,
    own, send, recv, ret, retsend, kset, vset, qin, din, qr, dor, dsb, pb, dqs, stats, gacc,
    part, parts, gsum,
    qsem, dsem, osem, fs, fr, bs, br, rs, rr, gs, gr, lsem,
):
    me = lax.axis_index("ctx")
    blocks = own.shape[0]
    g = gk_ref.shape[0]
    near = g + BLOCK
    shard = g // n
    barrier = pltpu.get_barrier_semaphore()

    def peer(i):
        return lax.rem(me + send_plan(i, n), n)

    def greet(i, carry):
        pl.semaphore_signal(barrier, inc=1, device_id={"ctx": peer(i)}, device_id_type=MESH)
        return carry

    lax.fori_loop(0, n - 1, greet, 0)

    def rows(b):
        return pl.ds(pl.multiple_of(b * BLOCK, BLOCK), BLOCK)

    def qcopy(b):
        return pltpu.make_async_copy(q_hbm.at[rows(b)], qin.at[b], qsem.at[b])

    def dcopy(b):
        return pltpu.make_async_copy(do_hbm.at[rows(b)], din.at[b], dsem.at[b])

    def ocopy(b):
        return pltpu.make_async_copy(dqs.at[b], dq_hbm.at[rows(b)], osem.at[b])

    def fetch(b, carry):
        qcopy(b).start()
        dcopy(b).start()
        return carry

    lax.fori_loop(0, blocks, fetch, 0)

    def turn(b, carry):
        own[b, :, :D] = rot(k_ref[rows(b)].astype(F32), c_ref[rows(b)], s_ref[rows(b)]).astype(BF16)
        own[b, :, D:] = v_ref[rows(b)]
        return carry

    lax.fori_loop(0, blocks, turn, 0)
    kset[:g] = gk_ref[...]
    vset[:g] = gv_ref[...]

    def pair(ref, i):
        return ref.at[pl.ds(pl.multiple_of(i * SLOTS, SLOTS), SLOTS)]

    def remote(src, dst, ssem, rsem, i):
        return pltpu.make_async_remote_copy(
            src, dst, ssem.at[i], rsem.at[i], device_id={"ctx": peer(i)}, device_id_type=MESH
        )

    def fcopy(i):
        return remote(pair(send, peer(i)), pair(recv, me), fs, fr, i)

    def bcopy(i):
        return remote(pair(retsend, peer(i)), pair(back_ref, me), bs, br, i)

    def rcopy(i):
        return remote(part.at[peer(i)], parts.at[me], rs, rr, i)

    def gcopy(i):
        return remote(gsum, glob_ref.at[me], gs, gr, i)

    def over(f):
        def body(i, carry):
            f(i)
            return carry

        lax.fori_loop(0, n - 1, body, 0)

    pl.semaphore_wait(barrier, n - 1)

    def give(i):
        to = peer(i)
        for j in range(SLOTS):
            send[to * SLOTS + j] = own[local_ref[to * SLOTS + j]]
        fcopy(i).start()

    over(give)
    for j in range(SLOTS):
        recv[me * SLOTS + j] = own[local_ref[me * SLOTS + j]]

    width = 256

    def near_stats(b, carry):
        qcopy(b).wait()
        dcopy(b).wait()
        kset[g:near] = own[b, :, :D]
        vset[g:near] = own[b, :, D:]
        c, s = c_ref[rows(b)], s_ref[rows(b)]
        for h in range(HEADS):
            at, cols = slice(h * BLOCK, (h + 1) * BLOCK), slice(h * D, (h + 1) * D)
            qr[b, at] = rot(qin[b, :, cols].astype(F32), c, s).astype(BF16)
            dor[b, at] = din[b, :, cols]
        for j in range(0, ROWS, width):
            at = slice(j, j + width)
            scores = dot(kset[:near], qr[b, at], NT)
            dp = dot(vset[:near], dor[b, at], NT)
            top = jnp.max(scores, axis=0, keepdims=True)
            e = jnp.exp2(scores * FACTOR2 - top * FACTOR2)
            stats[b, 0:1, at] = top
            stats[b, 1:2, at] = jnp.sum(e, axis=0, keepdims=True)
            stats[b, 2:3, at] = jnp.sum(e * dp, axis=0, keepdims=True)
        return carry

    lax.fori_loop(0, blocks, near_stats, 0)

    over(lambda i: fcopy(i).wait_recv())

    def far_pass(b, carry):
        fars = [recv[slot_ref[b * FAR + f]] for f in range(FAR)]
        fk = jnp.concatenate([x[:, :D] for x in fars], axis=0)
        fv = jnp.concatenate([x[:, D:] for x in fars], axis=0)
        scores = dot(fk, qr[b], NT)
        dp = dot(fv, dor[b], NT)
        top0 = stats[b, 0:1, :]
        top = jnp.maximum(jnp.max(scores, axis=0, keepdims=True), top0)
        shrink = jnp.exp2(top0 * FACTOR2 - top * FACTOR2)
        e = jnp.exp2(scores * FACTOR2 - top * FACTOR2)
        total = stats[b, 1:2, :] * shrink + jnp.sum(e, axis=0, keepdims=True)
        mixed = stats[b, 2:3, :] * shrink + jnp.sum(e * dp, axis=0, keepdims=True)
        w = 1.0 / total
        delta = mixed * w
        p = e * w
        stats[b, 3:4, :] = top * FACTOR2 + jnp.log(total) * math.log2(math.e)
        stats[b, 4:5, :] = delta
        ds = (p * (dp - delta)).astype(BF16)
        dsb[b, near:] = ds
        dk = dot(ds, qr[b], NN) * FACTOR
        dv = dot(p.astype(BF16), dor[b], NN)
        for f in range(FAR):
            at = slice(f * BLOCK, (f + 1) * BLOCK)
            ret[b * FAR + f, :, :D] = dk[at].astype(BF16)
            ret[b * FAR + f, :, D:] = dv[at].astype(BF16)
        return carry

    lax.fori_loop(0, blocks, far_pass, 0)

    def give_back(i):
        to = peer(i)
        for j in range(SLOTS):
            retsend[to * SLOTS + j] = ret[entry_ref[to * SLOTS + j]]
        bcopy(i).start()

    over(give_back)
    for j in range(SLOTS):
        retsend[me * SLOTS + j] = ret[entry_ref[me * SLOTS + j]]
    kept = pltpu.make_async_copy(pair(retsend, me), pair(back_ref, me), lsem.at[0])
    kept.start()

    gacc[...] = jnp.zeros_like(gacc)

    def near_pass(b, carry):
        kset[g:near] = own[b, :, :D]
        vset[g:near] = own[b, :, D:]
        for j in range(0, ROWS, width):
            at = slice(j, j + width)
            scores = dot(kset[:near], qr[b, at], NT)
            dp = dot(vset[:near], dor[b, at], NT)
            p = jnp.exp2(scores * FACTOR2 - stats[b, 3:4, at])
            pb[:, at] = p.astype(BF16)
            dsb[b, :near, at] = (p * (dp - stats[b, 4:5, at])).astype(BF16)
        dk = dot(dsb[b, :near], qr[b], NN) * FACTOR
        dv = dot(pb[...], dor[b], NN)
        gacc[:, :D] += dk[:g]
        gacc[:, D:] += dv[:g]
        dkv_ref[rows(b), :D] = dk[g:]
        dkv_ref[rows(b), D:] = dv[g:]
        return carry

    lax.fori_loop(0, blocks, near_pass, 0)
    for i in range(n):
        part[i] = gacc[i * shard : (i + 1) * shard].astype(BF16)
    over(lambda i: rcopy(i).start())
    parts[me] = part[me]

    def query_pass(b, carry):
        kset[g:near] = own[b, :, :D]
        for f in range(FAR):
            at = slice(near + f * BLOCK, near + (f + 1) * BLOCK)
            kset[at] = recv[slot_ref[b * FAR + f]][:, :D]
        dq = dot(dsb[b], kset[...], TN) * FACTOR
        for h in range(HEADS):
            dqs[b, :, h * D : (h + 1) * D] = dq[h * BLOCK : (h + 1) * BLOCK]
        ocopy(b).start()
        return carry

    lax.fori_loop(0, blocks, query_pass, 0)

    over(lambda i: rcopy(i).wait_recv())
    gsum[...] = jnp.sum(parts[...].astype(F32), axis=0).astype(BF16)
    over(lambda i: gcopy(i).start())
    mine = pltpu.make_async_copy(gsum, glob_ref.at[me], lsem.at[1])
    mine.start()
    over(lambda i: fcopy(i).wait_send())
    over(lambda i: rcopy(i).wait_send())
    over(lambda i: bcopy(i).wait())

    def drain(b, carry):
        ocopy(b).wait()
        return carry

    lax.fori_loop(0, blocks, drain, 0)
    kept.wait()
    mine.wait()
    over(lambda i: gcopy(i).wait())


def main(local, slots, entry, keys, values, c, s, gk, gv, q, do, n):
    tok = keys.shape[0]
    blocks = tok // BLOCK
    g = gk.shape[0]
    shard = g // n
    near = g + BLOCK
    smem, vmem, any_ = (pl.BlockSpec(memory_space=m) for m in (pltpu.SMEM, pltpu.VMEM, pl.ANY))
    dma = lambda k: pltpu.SemaphoreType.DMA((k,))
    return pl.pallas_call(
        functools.partial(main_kernel, n),
        in_specs=[smem] * 3 + [vmem] * 6 + [any_] * 2,
        out_specs=[any_, vmem, any_, any_],
        out_shape=[
            jax.ShapeDtypeStruct((tok, HEADS * D), F32),
            jax.ShapeDtypeStruct((tok, 2 * D), F32),
            jax.ShapeDtypeStruct((n * SLOTS, BLOCK, 2 * D), BF16),
            jax.ShapeDtypeStruct((n, shard, 2 * D), BF16),
        ],
        scratch_shapes=[
            pltpu.VMEM((blocks, BLOCK, 2 * D), BF16),
            pltpu.VMEM((n * SLOTS, BLOCK, 2 * D), BF16),
            pltpu.VMEM((n * SLOTS, BLOCK, 2 * D), BF16),
            pltpu.VMEM((blocks * FAR, BLOCK, 2 * D), BF16),
            pltpu.VMEM((n * SLOTS, BLOCK, 2 * D), BF16),
            pltpu.VMEM((near + FAR * BLOCK, D), BF16),
            pltpu.VMEM((near, D), BF16),
            pltpu.VMEM((blocks, BLOCK, HEADS * D), BF16),
            pltpu.VMEM((blocks, BLOCK, HEADS * D), BF16),
            pltpu.VMEM((blocks, ROWS, D), BF16),
            pltpu.VMEM((blocks, ROWS, D), BF16),
            pltpu.VMEM((blocks, near + FAR * BLOCK, ROWS), BF16),
            pltpu.VMEM((near, ROWS), BF16),
            pltpu.VMEM((blocks, BLOCK, HEADS * D), F32),
            pltpu.VMEM((blocks, 8, ROWS), F32),
            pltpu.VMEM((g, 2 * D), F32),
            pltpu.VMEM((n, shard, 2 * D), BF16),
            pltpu.VMEM((n, shard, 2 * D), BF16),
            pltpu.VMEM((shard, 2 * D), BF16),
            dma(blocks), dma(blocks), dma(blocks),
            dma(n), dma(n), dma(n), dma(n), dma(n), dma(n), dma(n), dma(n), dma(2),
        ],
        compiler_params=pltpu.CompilerParams(
            collective_id=0, has_side_effects=True, vmem_limit_bytes=56 << 20
        ),
        name="main",
    )(local, slots, entry, keys, values, c, s, gk, gv, q, do)


def final_kernel(
    local_ref, valid_ref, dq_ref, dkv_ref, back_ref, glob_ref, c_ref, s_ref,
    qg_ref, kg_ref, vg_ref, gk_ref, gv_ref, acc,
):
    b = pl.program_id(0)
    blocks = acc.shape[0]
    n, shard, _ = glob_ref.shape

    @pl.when(b == 0)
    def _():
        for i in range(blocks):
            acc[i] = dkv_ref[i * BLOCK : (i + 1) * BLOCK]

        def add(i, carry):
            @pl.when(valid_ref[i] > 0)
            def _():
                acc[local_ref[i]] += back_ref[i].astype(F32)

            return carry

        lax.fori_loop(0, back_ref.shape[0], add, 0)
        for i in range(n):
            gk_ref[i * shard : (i + 1) * shard] = glob_ref[i, :, :D].astype(F32)
            gv_ref[i * shard : (i + 1) * shard] = glob_ref[i, :, D:].astype(F32)

    c, s = c_ref[...], s_ref[...]
    for h in range(HEADS):
        cols = slice(h * D, (h + 1) * D)
        qg_ref[:, cols] = unrot(dq_ref[:, cols], c, s)
    kg_ref[...] = unrot(acc[b, :, :D], c, s)
    vg_ref[...] = acc[b, :, D:]


def final(local, valid, dq, dkv, back, glob, c, s):
    tok = dkv.shape[0]
    blocks = tok // BLOCK
    n, shard, _ = glob.shape
    tile = lambda b: (b, 0)
    whole2 = lambda b: (0, 0)
    whole3 = lambda b: (0, 0, 0)
    return pl.pallas_call(
        final_kernel,
        grid=(blocks,),
        in_specs=[
            pl.BlockSpec(memory_space=pltpu.SMEM),
            pl.BlockSpec(memory_space=pltpu.SMEM),
            pl.BlockSpec((BLOCK, HEADS * D), tile),
            pl.BlockSpec((tok, 2 * D), whole2),
            pl.BlockSpec(back.shape, whole3),
            pl.BlockSpec(glob.shape, whole3),
            pl.BlockSpec((BLOCK, D), tile),
            pl.BlockSpec((BLOCK, D), tile),
        ],
        out_specs=[
            pl.BlockSpec((BLOCK, HEADS * D), tile),
            pl.BlockSpec((BLOCK, D), tile),
            pl.BlockSpec((BLOCK, D), tile),
            pl.BlockSpec((n * shard, D), whole2),
            pl.BlockSpec((n * shard, D), whole2),
        ],
        out_shape=[
            jax.ShapeDtypeStruct((tok, HEADS * D), F32),
            jax.ShapeDtypeStruct((tok, D), F32),
            jax.ShapeDtypeStruct((tok, D), F32),
            jax.ShapeDtypeStruct((n * shard, D), F32),
            jax.ShapeDtypeStruct((n * shard, D), F32),
        ],
        scratch_shapes=[pltpu.VMEM((blocks, BLOCK, 2 * D), F32)],
        compiler_params=pltpu.CompilerParams(vmem_limit_bytes=32 << 20),
        name="final",
    )(local, valid, dq, dkv, back, glob, c, s)


def on_device(queries, keys, values, dout, glob_keys, glob_values, frames, far_owner, far_local):
    n = lax.axis_size("ctx")
    me = lax.axis_index("ctx")
    blocks = keys.shape[0] // BLOCK
    entries = blocks * FAR
    c, s = rotary_tables(frames)
    owners = far_owner.reshape(n, entries)
    locals_ = far_local.reshape(n, entries)
    place = jnp.arange(entries)
    rank = jnp.sum(
        (owners[:, :, None] == owners[:, None, :]) & (place[None, :] < place[:, None]), axis=-1
    )
    slots = lax.dynamic_index_in_dim(owners * SLOTS + rank, me, 0, keepdims=False)
    chosen = (owners == me)[:, None, :] & (rank[:, None, :] == jnp.arange(SLOTS)[None, :, None])
    local = jnp.sum(jnp.where(chosen, locals_[:, None, :], 0), axis=-1).reshape(-1)
    valid = jnp.sum(chosen.astype(jnp.int32), axis=-1).reshape(-1)

    entry = jnp.sum(
        jnp.where(slots[None, :] == jnp.arange(n * SLOTS)[:, None], place[None, :], 0), axis=-1
    )

    dq, dkv, back, glob = main(
        local, slots, entry, keys, values, c, s, glob_keys, glob_values, queries, dout, n
    )
    return final(local, valid, dq, dkv, back, glob, c, s)


def solution(mesh):
    both = P(("grp", "ctx"), None)
    one = P("grp", None)
    return jax.shard_map(
        on_device,
        mesh=mesh,
        in_specs=(both, both, both, both, one, one, P(("grp", "ctx")), one, one),
        out_specs=(both, both, both, one, one),
        check_vma=False,
    )
```

```python
import functools
import math

import jax
import jax.numpy as jnp
from jax import lax
from jax.experimental import pallas as pl
from jax.experimental.pallas import tpu as pltpu
from jax.sharding import PartitionSpec as P

F32, BF16 = jnp.float32, jnp.bfloat16
MESH = pl.DeviceIdType.MESH
BLOCK, FAR, SLOTS, D, HEADS = 64, 2, 2, 128, 8
ROWS = BLOCK * HEADS

rope_base = 1000000.0
yarn_factor = 4.0
orig_context = 32768.0
ramp_low = 1.0
ramp_high = 32.0

FACTOR = (0.1 * math.log(yarn_factor) + 1.0) ** 2 / math.sqrt(D)
FACTOR2 = FACTOR * math.log2(math.e)

NT = (((1,), (1,)), ((), ()))
NN = (((1,), (0,)), ((), ()))
TN = (((0,), (0,)), ((), ()))


def dot(a, b, dims):
    return lax.dot_general(a, b, dims, preferred_element_type=F32)


def rotary_tables(frame_ids):
    half = D // 2
    index = jnp.arange(half).astype(F32)
    inverse = rope_base ** (-2.0 * index / D)
    ratios = orig_context * inverse / (2.0 * math.pi)
    ramp = jnp.clip((ratios - ramp_low) / (ramp_high - ramp_low), 0.0, 1.0)
    frequency = inverse * ((1.0 - ramp) / yarn_factor + ramp)
    twice = jnp.concatenate([frequency, frequency])
    signed = jnp.concatenate([-frequency, frequency])
    at = frame_ids.astype(F32)[:, None]
    return jnp.cos(at * twice[None, :]), jnp.sin(at * signed[None, :])


def rot(x, c, s):
    return x * c + pltpu.roll(x, D // 2, 1) * s


def unrot(x, c, s):
    return x * c - pltpu.roll(x, D // 2, 1) * s


def send_plan(i, n):
    return 1 + lax.rem(i * 11, n - 1)


def main_kernel(
    n, owner_ref, place_ref, k_ref, v_ref, c_ref, s_ref, gk_ref, gv_ref, q_hbm, do_hbm,
    dq_hbm, dkv_hbm, backk_ref, backv_ref, glob_ref, index_ref,
    ownk, ownv, sendk, sendv, recvk, recvv, retk, retv, rsendk, rsendv,
    kset, vset, qin, din, qr, dor, dsb, pb, pfar, dqs, dkvs, stats, gacc, part, parts, gsum,
    entry, slot,
    qsem, dsem, osem, kfs, kfr, vfs, vfr, kbs, kbr, vbs, vbr, rs, rr, gs, gr, lsem,
):
    me = lax.axis_index("ctx")
    blocks = ownk.shape[0]
    g = gk_ref.shape[0]
    near = g + BLOCK
    shard = g // n
    barrier = pltpu.get_barrier_semaphore()

    def peer(i):
        return lax.rem(me + send_plan(i, n), n)

    def over(f, count=n - 1):
        def body(i, carry):
            f(i)
            return carry

        lax.fori_loop(0, count, body, 0)

    over(
        lambda i: pl.semaphore_signal(
            barrier, inc=1, device_id={"ctx": peer(i)}, device_id_type=MESH
        )
    )

    def rows(b):
        return pl.ds(pl.multiple_of(b * BLOCK, BLOCK), BLOCK)

    def qcopy(b):
        return pltpu.make_async_copy(q_hbm.at[rows(b)], qin.at[b], qsem.at[b])

    def dcopy(b):
        return pltpu.make_async_copy(do_hbm.at[rows(b)], din.at[b], dsem.at[b])

    def ocopy(b):
        return pltpu.make_async_copy(dqs.at[b], dq_hbm.at[rows(b)], osem.at[b])

    def fetch(b):
        qcopy(b).start()
        dcopy(b).start()

    over(fetch, blocks)

    def turn(b):
        x = k_ref[rows(b)].astype(F32)
        ownk[b] = rot(x, c_ref[rows(b)], s_ref[rows(b)]).astype(BF16)
        ownv[b] = v_ref[rows(b)]

    over(turn, blocks)

    def find(row, wanted, value):
        first, second, count = jnp.int32(0), jnp.int32(0), jnp.int32(0)
        for f in range(FAR):
            for b in range(blocks):
                hit = owner_ref[f, row * blocks + b] == wanted
                v = value(f, b)
                first = jnp.where(hit & (count == 0), v, first)
                second = jnp.where(hit & (count == 1), v, second)
                count = count + hit.astype(jnp.int32)
        return first, second, count

    total_slots = n * SLOTS

    def listed(d):
        found = find(d, me, lambda f, b: place_ref[f, d * blocks + b])
        for j in range(SLOTS):
            index_ref[d * SLOTS + j] = found[j]
            index_ref[total_slots + d * SLOTS + j] = (found[2] > j).astype(jnp.int32)

    over(listed, n)

    def pair(ref, i):
        return ref.at[pl.ds(pl.multiple_of(i * SLOTS, SLOTS), SLOTS)]

    def remote(src, dst, ssem, rsem, i):
        return pltpu.make_async_remote_copy(
            src, dst, ssem.at[i], rsem.at[i], device_id={"ctx": peer(i)}, device_id_type=MESH
        )

    def kcopy(i):
        return remote(pair(sendk, peer(i)), pair(recvk, me), kfs, kfr, i)

    def vcopy(i):
        return remote(pair(sendv, peer(i)), pair(recvv, me), vfs, vfr, i)

    def kback(i):
        return remote(pair(rsendk, peer(i)), pair(backk_ref, me), kbs, kbr, i)

    def vback(i):
        return remote(pair(rsendv, peer(i)), pair(backv_ref, me), vbs, vbr, i)

    def rcopy(i):
        return remote(part.at[peer(i)], parts.at[me], rs, rr, i)

    def gcopy(i):
        return remote(gsum, glob_ref.at[me], gs, gr, i)

    def lay(dst, src, to, table):
        for j in range(SLOTS):
            dst[to * SLOTS + j] = src[table[to * SLOTS + j]]

    pl.semaphore_wait(barrier, n - 1)

    def give_k(i):
        lay(sendk, ownk, peer(i), index_ref)
        kcopy(i).start()

    def give_v(i):
        lay(sendv, ownv, peer(i), index_ref)
        vcopy(i).start()

    over(give_k)
    over(give_v)
    lay(recvk, ownk, me, index_ref)
    lay(recvv, ownv, me, index_ref)

    def mine(o):
        found = find(me, o, lambda f, b: jnp.int32(b * FAR + f))
        for j in range(SLOTS):
            entry[o * SLOTS + j] = found[j]

    over(mine, n)

    def seat(b):
        for f in range(FAR):
            o = owner_ref[f, me * blocks + b]
            second = entry[o * SLOTS + 1] == b * FAR + f
            several = entry[o * SLOTS] != b * FAR + f
            slot[b * FAR + f] = o * SLOTS + (second & several).astype(jnp.int32)

    over(seat, blocks)

    kset[:g] = gk_ref[...]
    vset[:g] = gv_ref[...]
    width = 256

    def near_stats(b):
        qcopy(b).wait()
        dcopy(b).wait()
        kset[g:near] = ownk[b]
        vset[g:near] = ownv[b]
        c, s = c_ref[rows(b)], s_ref[rows(b)]
        for h in range(HEADS):
            at, cols = slice(h * BLOCK, (h + 1) * BLOCK), slice(h * D, (h + 1) * D)
            qr[b, at] = rot(qin[b, :, cols].astype(F32), c, s).astype(BF16)
            dor[b, at] = din[b, :, cols]
        for j in range(0, ROWS, width):
            at = slice(j, j + width)
            scores = dot(kset[:near], qr[b, at], NT)
            dp = dot(vset[:near], dor[b, at], NT)
            top = jnp.max(scores, axis=0, keepdims=True)
            e = jnp.exp2(scores * FACTOR2 - top * FACTOR2)
            stats[b, 0:1, at] = top
            stats[b, 1:2, at] = jnp.sum(e, axis=0, keepdims=True)
            stats[b, 2:3, at] = jnp.sum(e * dp, axis=0, keepdims=True)

    over(near_stats, blocks)

    over(lambda i: kcopy(i).wait_recv())

    def halves(x):
        return [x[f * BLOCK : (f + 1) * BLOCK] for f in range(FAR)]

    def far_values(b):
        fk = jnp.concatenate([recvk[slot[b * FAR + f]] for f in range(FAR)], axis=0)
        scores = dot(fk, qr[b], NT)
        top0 = stats[b, 0:1, :]
        top = jnp.maximum(jnp.max(scores, axis=0, keepdims=True), top0)
        shrink = jnp.exp2(top0 * FACTOR2 - top * FACTOR2)
        e = jnp.exp2(scores * FACTOR2 - top * FACTOR2)
        total = stats[b, 1:2, :] * shrink + jnp.sum(e, axis=0, keepdims=True)
        w = 1.0 / total
        p = e * w
        pfar[b] = p
        stats[b, 3:4, :] = top * FACTOR2 + jnp.log(total) * math.log2(math.e)
        stats[b, 4:5, :] = stats[b, 2:3, :] * shrink * w
        for f, x in enumerate(halves(dot(p.astype(BF16), dor[b], NN))):
            retv[b * FAR + f] = x.astype(BF16)

    over(far_values, blocks)

    def return_v(i):
        lay(rsendv, retv, peer(i), entry)
        vback(i).start()

    over(return_v)

    over(lambda i: vcopy(i).wait_recv())

    def far_keys(b):
        fv = jnp.concatenate([recvv[slot[b * FAR + f]] for f in range(FAR)], axis=0)
        dp = dot(fv, dor[b], NT)
        p = pfar[b]
        delta = stats[b, 4:5, :] + jnp.sum(p * dp, axis=0, keepdims=True)
        stats[b, 5:6, :] = delta
        ds = (p * (dp - delta)).astype(BF16)
        dsb[b, near:] = ds
        for f, x in enumerate(halves(dot(ds, qr[b], NN) * FACTOR)):
            retk[b * FAR + f] = x.astype(BF16)

    over(far_keys, blocks)

    def return_k(i):
        lay(rsendk, retk, peer(i), entry)
        kback(i).start()

    over(return_k)
    lay(rsendk, retk, me, entry)
    lay(rsendv, retv, me, entry)
    keptk = pltpu.make_async_copy(pair(rsendk, me), pair(backk_ref, me), lsem.at[0])
    keptv = pltpu.make_async_copy(pair(rsendv, me), pair(backv_ref, me), lsem.at[1])
    keptk.start()
    keptv.start()

    gacc[...] = jnp.zeros_like(gacc)

    def near_pass(b):
        kset[g:near] = ownk[b]
        vset[g:near] = ownv[b]
        for j in range(0, ROWS, width):
            at = slice(j, j + width)
            scores = dot(kset[:near], qr[b, at], NT)
            dp = dot(vset[:near], dor[b, at], NT)
            p = jnp.exp2(scores * FACTOR2 - stats[b, 3:4, at])
            pb[:, at] = p.astype(BF16)
            dsb[b, :near, at] = (p * (dp - stats[b, 5:6, at])).astype(BF16)
        dk = dot(dsb[b, :near], qr[b], NN) * FACTOR
        dv = dot(pb[...], dor[b], NN)
        gacc[:, :D] += dk[:g]
        gacc[:, D:] += dv[:g]
        dkvs[b, :, :D] = dk[g:]
        dkvs[b, :, D:] = dv[g:]

    over(near_pass, blocks)
    for i in range(n):
        part[i] = gacc[i * shard : (i + 1) * shard].astype(BF16)
    over(lambda i: rcopy(i).start())
    parts[me] = part[me]
    owned = pltpu.make_async_copy(dkvs, dkv_hbm, lsem.at[2])
    owned.start()

    def query_pass(b):
        kset[g:near] = ownk[b]
        for f in range(FAR):
            kset[near + f * BLOCK : near + (f + 1) * BLOCK] = recvk[slot[b * FAR + f]]
        dq = dot(dsb[b], kset[...], TN) * FACTOR
        c, s = c_ref[rows(b)], s_ref[rows(b)]
        for h in range(HEADS):
            dqs[b, :, h * D : (h + 1) * D] = unrot(dq[h * BLOCK : (h + 1) * BLOCK], c, s)
        ocopy(b).start()

    over(query_pass, blocks)

    over(lambda i: rcopy(i).wait_recv())
    gsum[...] = jnp.sum(parts[...].astype(F32), axis=0).astype(BF16)
    over(lambda i: gcopy(i).start())
    kept = pltpu.make_async_copy(gsum, glob_ref.at[me], lsem.at[3])
    kept.start()
    over(lambda i: kcopy(i).wait_send())
    over(lambda i: vcopy(i).wait_send())
    over(lambda i: rcopy(i).wait_send())
    over(lambda b: ocopy(b).wait(), blocks)
    owned.wait()
    keptk.wait()
    keptv.wait()
    kept.wait()
    over(lambda i: vback(i).wait())
    over(lambda i: kback(i).wait())
    over(lambda i: gcopy(i).wait())


def main(owner, place, keys, values, c, s, gk, gv, q, do, n):
    tok = keys.shape[0]
    blocks = tok // BLOCK
    g = gk.shape[0]
    shard = g // n
    near = g + BLOCK
    smem, vmem, any_ = (pl.BlockSpec(memory_space=m) for m in (pltpu.SMEM, pltpu.VMEM, pl.ANY))
    dma = lambda k: pltpu.SemaphoreType.DMA((k,))
    slots = pltpu.VMEM((n * SLOTS, BLOCK, D), BF16)
    mine = pltpu.VMEM((blocks, BLOCK, D), BF16)
    ends = pltpu.VMEM((blocks * FAR, BLOCK, D), BF16)
    return pl.pallas_call(
        functools.partial(main_kernel, n),
        in_specs=[smem] * 2 + [vmem] * 6 + [any_] * 2,
        out_specs=[any_] * 5 + [smem],
        out_shape=[
            jax.ShapeDtypeStruct((tok, HEADS * D), F32),
            jax.ShapeDtypeStruct((blocks, BLOCK, 2 * D), F32),
            jax.ShapeDtypeStruct((n * SLOTS, BLOCK, D), BF16),
            jax.ShapeDtypeStruct((n * SLOTS, BLOCK, D), BF16),
            jax.ShapeDtypeStruct((n, shard, 2 * D), BF16),
            jax.ShapeDtypeStruct((2 * n * SLOTS,), jnp.int32),
        ],
        scratch_shapes=[
            mine, mine, slots, slots, slots, slots, ends, ends, slots, slots,
            pltpu.VMEM((near + FAR * BLOCK, D), BF16),
            pltpu.VMEM((near, D), BF16),
            pltpu.VMEM((blocks, BLOCK, HEADS * D), BF16),
            pltpu.VMEM((blocks, BLOCK, HEADS * D), BF16),
            pltpu.VMEM((blocks, ROWS, D), BF16),
            pltpu.VMEM((blocks, ROWS, D), BF16),
            pltpu.VMEM((blocks, near + FAR * BLOCK, ROWS), BF16),
            pltpu.VMEM((near, ROWS), BF16),
            pltpu.VMEM((blocks, FAR * BLOCK, ROWS), F32),
            pltpu.VMEM((blocks, BLOCK, HEADS * D), F32),
            pltpu.VMEM((blocks, BLOCK, 2 * D), F32),
            pltpu.VMEM((blocks, 8, ROWS), F32),
            pltpu.VMEM((g, 2 * D), F32),
            pltpu.VMEM((n, shard, 2 * D), BF16),
            pltpu.VMEM((n, shard, 2 * D), BF16),
            pltpu.VMEM((shard, 2 * D), BF16),
            pltpu.SMEM((n * SLOTS,), jnp.int32),
            pltpu.SMEM((blocks * FAR,), jnp.int32),
            dma(blocks), dma(blocks), dma(blocks),
        ] + [dma(n)] * 12 + [dma(4)],
        compiler_params=pltpu.CompilerParams(
            collective_id=0, has_side_effects=True, vmem_limit_bytes=58 << 20
        ),
        name="main",
    )(owner, place, keys, values, c, s, gk, gv, q, do)


def final_kernel(
    index_ref, dq_hbm, acc_ref, backk_ref, backv_ref, glob_ref, c_ref, s_ref,
    qg_hbm, kg_ref, vg_ref, gk_ref, gv_ref, acc, sem,
):
    blocks = acc.shape[0]
    n, shard, _ = glob_ref.shape
    total = backk_ref.shape[0]
    tok = blocks * BLOCK
    pieces = sem.shape[0]
    step = tok // pieces
    moves = [
        pltpu.make_async_copy(
            dq_hbm.at[pl.ds(i * step, step)], qg_hbm.at[pl.ds(i * step, step)], sem.at[i]
        )
        for i in range(pieces)
    ]
    for m in moves:
        m.start()
    acc[...] = acc_ref[...]

    def add(i, carry):
        @pl.when(index_ref[total + i] > 0)
        def _():
            at = index_ref[i]
            acc[at, :, :D] += backk_ref[i].astype(F32)
            acc[at, :, D:] += backv_ref[i].astype(F32)

        return carry

    lax.fori_loop(0, total, add, 0)
    for b in range(blocks):
        r = slice(b * BLOCK, (b + 1) * BLOCK)
        kg_ref[r] = unrot(acc[b, :, :D], c_ref[r], s_ref[r])
        vg_ref[r] = acc[b, :, D:]
    for i in range(n):
        gk_ref[i * shard : (i + 1) * shard] = glob_ref[i, :, :D].astype(F32)
        gv_ref[i * shard : (i + 1) * shard] = glob_ref[i, :, D:].astype(F32)
    for m in moves:
        m.wait()


def final(index, dq, dkv, backk, backv, glob, c, s):
    blocks = dkv.shape[0]
    tok = blocks * BLOCK
    n, shard, _ = glob.shape
    smem, vmem, any_ = (pl.BlockSpec(memory_space=m) for m in (pltpu.SMEM, pltpu.VMEM, pl.ANY))
    return pl.pallas_call(
        final_kernel,
        in_specs=[smem, any_] + [vmem] * 6,
        out_specs=[any_] + [vmem] * 4,
        out_shape=[
            jax.ShapeDtypeStruct((tok, HEADS * D), F32),
            jax.ShapeDtypeStruct((tok, D), F32),
            jax.ShapeDtypeStruct((tok, D), F32),
            jax.ShapeDtypeStruct((n * shard, D), F32),
            jax.ShapeDtypeStruct((n * shard, D), F32),
        ],
        scratch_shapes=[
            pltpu.VMEM((blocks, BLOCK, 2 * D), F32),
            pltpu.SemaphoreType.DMA((8,)),
        ],
        compiler_params=pltpu.CompilerParams(vmem_limit_bytes=60 << 20),
        name="final",
    )(index, dq, dkv, backk, backv, glob, c, s)


def on_device(queries, keys, values, dout, glob_keys, glob_values, frames, far_owner, far_local):
    n = lax.axis_size("ctx")
    c, s = rotary_tables(frames)
    dq, dkv, backk, backv, glob, index = main(
        far_owner.T, far_local.T, keys, values, c, s, glob_keys, glob_values, queries, dout, n
    )
    return tuple(final(index, dq, dkv, backk, backv, glob, c, s))


def solution(mesh):
    both = P(("grp", "ctx"), None)
    one = P("grp", None)
    return jax.shard_map(
        on_device,
        mesh=mesh,
        in_specs=(both, both, both, both, one, one, P(("grp", "ctx")), one, one),
        out_specs=(both, both, both, one, one),
        check_vma=False,
    )
```

```python
import functools
import math

import jax
import jax.numpy as jnp
import numpy as np
from jax import lax
from jax.experimental import pallas as pl
from jax.experimental.pallas import tpu as pltpu
from jax.sharding import PartitionSpec as P

F32, BF16 = jnp.float32, jnp.bfloat16
MESH = pl.DeviceIdType.MESH
BLOCK, FAR, SLOTS, D, HEADS = 64, 2, 2, 128, 8
ROWS = BLOCK * HEADS

rope_base = 1000000.0
yarn_factor = 4.0
orig_context = 32768.0
ramp_low = 1.0
ramp_high = 32.0

FACTOR = (0.1 * math.log(yarn_factor) + 1.0) ** 2 / math.sqrt(D)
FACTOR2 = FACTOR * math.log2(math.e)

LANES = 128

NT = (((1,), (1,)), ((), ()))
NN = (((1,), (0,)), ((), ()))
TN = (((0,), (0,)), ((), ()))


def dot(a, b, dims):
    return lax.dot_general(a, b, dims, preferred_element_type=F32)


def frequencies():
    index = np.arange(D // 2, dtype=np.float64)
    inverse = rope_base ** (-2.0 * index / D)
    ratios = orig_context * inverse / (2.0 * math.pi)
    ramp = np.clip((ratios - ramp_low) / (ramp_high - ramp_low), 0.0, 1.0)
    frequency = inverse * ((1.0 - ramp) / yarn_factor + ramp)
    return np.concatenate([frequency, frequency])[None, :].astype(np.float32)


def rot(x, c, s):
    return x * c + pltpu.roll(x, D // 2, 1) * s


def unrot(x, c, s):
    return x * c - pltpu.roll(x, D // 2, 1) * s


def send_plan(i, n):
    return 1 + lax.rem(i * 11, n - 1)


def main_kernel(
    n, owner_ref, place_ref, frame_ref, freq_ref, k_ref, v_ref, gk_ref, gv_ref, q_hbm, do_hbm,
    dq_hbm, dkv_hbm, backk_ref, backv_ref, glob_ref, c_hbm, s_hbm, index_ref,
    c_ref, s_ref,
    ownk, ownv, sendk, sendv, recvk, recvv, retk, retv, rsendk, rsendv,
    kset, vset, qin, din, qr, dor, dsb, pb, pfar, dqs, dkvs, stats, gacc, part, parts, gsum,
    entry, slot,
    qsem, dsem, osem, kfs, kfr, vfs, vfr, kbs, kbr, vbs, vbr, rs, rr, gs, gr, lsem,
):
    me = lax.axis_index("ctx")
    blocks = ownk.shape[0]
    g = gk_ref.shape[0]
    near = g + BLOCK
    shard = g // n
    barrier = pltpu.get_barrier_semaphore()

    def peer(i):
        return lax.rem(me + send_plan(i, n), n)

    def over(f, count=n - 1):
        def body(i, carry):
            f(i)
            return carry

        lax.fori_loop(0, count, body, 0)

    over(
        lambda i: pl.semaphore_signal(
            barrier, inc=1, device_id={"ctx": peer(i)}, device_id_type=MESH
        )
    )

    def rows(b):
        return pl.ds(pl.multiple_of(b * BLOCK, BLOCK), BLOCK)

    def qcopy(b):
        return pltpu.make_async_copy(q_hbm.at[rows(b)], qin.at[b], qsem.at[b])

    def dcopy(b):
        return pltpu.make_async_copy(do_hbm.at[rows(b)], din.at[b], dsem.at[b])

    def ocopy(b):
        return pltpu.make_async_copy(dqs.at[b], dq_hbm.at[rows(b)], osem.at[b])

    def fetch(b):
        qcopy(b).start()
        dcopy(b).start()

    over(fetch, blocks)

    half = blocks * BLOCK // 2
    low = lax.broadcasted_iota(jnp.int32, (LANES, LANES), 1) < D // 2
    for i in range(half // LANES):
        spread = [
            jnp.broadcast_to(frame_ref[j : j + 1].astype(F32), (LANES, LANES)).T
            for j in (i, i + half // LANES)
        ]
        angle = jnp.where(low, spread[0], spread[1]) * freq_ref[...]
        cosine, sine = jnp.cos(angle), jnp.sin(angle)
        cturn, sturn = pltpu.roll(cosine, D // 2, 1), pltpu.roll(sine, D // 2, 1)
        r0 = slice(i * LANES, (i + 1) * LANES)
        r1 = slice(half + i * LANES, half + (i + 1) * LANES)
        c_ref[r0] = jnp.where(low, cosine, cturn)
        s_ref[r0] = jnp.where(low, -sine, sturn)
        c_ref[r1] = jnp.where(low, cturn, cosine)
        s_ref[r1] = jnp.where(low, -sturn, sine)
    tables = [
        pltpu.make_async_copy(c_ref, c_hbm, lsem.at[4]),
        pltpu.make_async_copy(s_ref, s_hbm, lsem.at[5]),
    ]
    for t in tables:
        t.start()

    def turn(b):
        x = k_ref[rows(b)].astype(F32)
        ownk[b] = rot(x, c_ref[rows(b)], s_ref[rows(b)]).astype(BF16)
        ownv[b] = v_ref[rows(b)]

    over(turn, blocks)

    def find(row, wanted, value):
        first = second = jnp.int32(-1)
        for b in reversed(range(blocks)):
            for f in reversed(range(FAR)):
                hit = owner_ref[f, row * blocks + b] == wanted
                second = jnp.where(hit, first, second)
                first = jnp.where(hit, value(f, b), first)
        return first, second

    def listed(d):
        for j, x in enumerate(find(d, me, lambda f, b: place_ref[f, d * blocks + b])):
            index_ref[d * SLOTS + j] = x

    def pair(ref, i):
        return ref.at[pl.ds(pl.multiple_of(i * SLOTS, SLOTS), SLOTS)]

    def remote(src, dst, ssem, rsem, i):
        return pltpu.make_async_remote_copy(
            src, dst, ssem.at[i], rsem.at[i], device_id={"ctx": peer(i)}, device_id_type=MESH
        )

    def kcopy(i):
        return remote(pair(sendk, peer(i)), pair(recvk, me), kfs, kfr, i)

    def vcopy(i):
        return remote(pair(sendv, peer(i)), pair(recvv, me), vfs, vfr, i)

    def kback(i):
        return remote(pair(rsendk, peer(i)), pair(backk_ref, me), kbs, kbr, i)

    def vback(i):
        return remote(pair(rsendv, peer(i)), pair(backv_ref, me), vbs, vbr, i)

    def rcopy(i):
        return remote(part.at[peer(i)], parts.at[me], rs, rr, i)

    def gcopy(i):
        return remote(gsum, glob_ref.at[me], gs, gr, i)

    def lay(dst, src, to, table):
        for j in range(SLOTS):
            dst[to * SLOTS + j] = src[jnp.maximum(table[to * SLOTS + j], 0)]

    pl.semaphore_wait(barrier, n - 1)

    def give_k(i):
        listed(peer(i))
        lay(sendk, ownk, peer(i), index_ref)
        kcopy(i).start()

    def give_v(i):
        lay(sendv, ownv, peer(i), index_ref)
        vcopy(i).start()

    over(give_k)
    over(give_v)
    listed(me)
    lay(recvk, ownk, me, index_ref)
    lay(recvv, ownv, me, index_ref)

    def mine(o):
        for j, x in enumerate(find(me, o, lambda f, b: jnp.int32(b * FAR + f))):
            entry[o * SLOTS + j] = x

    over(mine, n)

    def seat(b):
        for f in range(FAR):
            o = owner_ref[f, me * blocks + b]
            later = entry[o * SLOTS] != b * FAR + f
            slot[b * FAR + f] = o * SLOTS + later.astype(jnp.int32)

    over(seat, blocks)

    kset[:g] = gk_ref[...]
    vset[:g] = gv_ref[...]
    width = 256

    def near_stats(b):
        qcopy(b).wait()
        dcopy(b).wait()
        kset[g:near] = ownk[b]
        vset[g:near] = ownv[b]
        c, s = c_ref[rows(b)], s_ref[rows(b)]
        for h in range(HEADS):
            at, cols = slice(h * BLOCK, (h + 1) * BLOCK), slice(h * D, (h + 1) * D)
            qr[b, at] = rot(qin[b, :, cols].astype(F32), c, s).astype(BF16)
            dor[b, at] = din[b, :, cols]
        for j in range(0, ROWS, width):
            at = slice(j, j + width)
            scores = dot(kset[:near], qr[b, at], NT)
            dp = dot(vset[:near], dor[b, at], NT)
            top = jnp.max(scores, axis=0, keepdims=True)
            e = jnp.exp2(scores * FACTOR2 - top * FACTOR2)
            stats[b, 0:1, at] = top
            stats[b, 1:2, at] = jnp.sum(e, axis=0, keepdims=True)
            stats[b, 2:3, at] = jnp.sum(e * dp, axis=0, keepdims=True)

    over(near_stats, blocks)

    over(lambda i: kcopy(i).wait_recv())

    def halves(x):
        return [x[f * BLOCK : (f + 1) * BLOCK] for f in range(FAR)]

    def far_values(b):
        fk = jnp.concatenate([recvk[slot[b * FAR + f]] for f in range(FAR)], axis=0)
        scores = dot(fk, qr[b], NT)
        top0 = stats[b, 0:1, :]
        top = jnp.maximum(jnp.max(scores, axis=0, keepdims=True), top0)
        shrink = jnp.exp2(top0 * FACTOR2 - top * FACTOR2)
        e = jnp.exp2(scores * FACTOR2 - top * FACTOR2)
        total = stats[b, 1:2, :] * shrink + jnp.sum(e, axis=0, keepdims=True)
        w = 1.0 / total
        p = e * w
        pfar[b] = p
        stats[b, 3:4, :] = top * FACTOR2 + jnp.log(total) * math.log2(math.e)
        stats[b, 4:5, :] = stats[b, 2:3, :] * shrink * w
        for f, x in enumerate(halves(dot(p.astype(BF16), dor[b], NN))):
            retv[b * FAR + f] = x.astype(BF16)

    over(far_values, blocks)

    def return_v(i):
        lay(rsendv, retv, peer(i), entry)
        vback(i).start()

    over(return_v)

    over(lambda i: vcopy(i).wait_recv())

    def far_keys(b):
        fv = jnp.concatenate([recvv[slot[b * FAR + f]] for f in range(FAR)], axis=0)
        dp = dot(fv, dor[b], NT)
        p = pfar[b]
        delta = stats[b, 4:5, :] + jnp.sum(p * dp, axis=0, keepdims=True)
        stats[b, 5:6, :] = delta
        ds = (p * (dp - delta)).astype(BF16)
        dsb[b, near:] = ds
        for f, x in enumerate(halves(dot(ds, qr[b], NN) * FACTOR)):
            retk[b * FAR + f] = x.astype(BF16)

    over(far_keys, blocks)

    def return_k(i):
        lay(rsendk, retk, peer(i), entry)
        kback(i).start()

    over(return_k)
    lay(rsendk, retk, me, entry)
    lay(rsendv, retv, me, entry)
    keptk = pltpu.make_async_copy(pair(rsendk, me), pair(backk_ref, me), lsem.at[0])
    keptv = pltpu.make_async_copy(pair(rsendv, me), pair(backv_ref, me), lsem.at[1])
    keptk.start()
    keptv.start()

    gacc[...] = jnp.zeros_like(gacc)

    def near_pass(b):
        kset[g:near] = ownk[b]
        vset[g:near] = ownv[b]
        for j in range(0, ROWS, width):
            at = slice(j, j + width)
            scores = dot(kset[:near], qr[b, at], NT)
            dp = dot(vset[:near], dor[b, at], NT)
            p = jnp.exp2(scores * FACTOR2 - stats[b, 3:4, at])
            pb[:, at] = p.astype(BF16)
            dsb[b, :near, at] = (p * (dp - stats[b, 5:6, at])).astype(BF16)
        dk = dot(dsb[b, :near], qr[b], NN) * FACTOR
        dv = dot(pb[...], dor[b], NN)
        gacc[:, :D] += dk[:g]
        gacc[:, D:] += dv[:g]
        dkvs[b, :, :D] = dk[g:]
        dkvs[b, :, D:] = dv[g:]

    over(near_pass, blocks)
    for i in range(n):
        part[i] = gacc[i * shard : (i + 1) * shard].astype(BF16)
    over(lambda i: rcopy(i).start())
    parts[me] = part[me]
    owned = pltpu.make_async_copy(dkvs, dkv_hbm, lsem.at[2])
    owned.start()

    def query_pass(b):
        kset[g:near] = ownk[b]
        for f in range(FAR):
            kset[near + f * BLOCK : near + (f + 1) * BLOCK] = recvk[slot[b * FAR + f]]
        dq = dot(dsb[b], kset[...], TN) * FACTOR
        c, s = c_ref[rows(b)], s_ref[rows(b)]
        for h in range(HEADS):
            dqs[b, :, h * D : (h + 1) * D] = unrot(dq[h * BLOCK : (h + 1) * BLOCK], c, s)
        ocopy(b).start()

    over(query_pass, blocks)

    over(lambda i: rcopy(i).wait_recv())
    gsum[...] = jnp.sum(parts[...].astype(F32), axis=0).astype(BF16)
    over(lambda i: gcopy(i).start())
    kept = pltpu.make_async_copy(gsum, glob_ref.at[me], lsem.at[3])
    kept.start()
    over(lambda i: kcopy(i).wait_send())
    over(lambda i: vcopy(i).wait_send())
    over(lambda i: rcopy(i).wait_send())
    over(lambda b: ocopy(b).wait(), blocks)
    for t in tables:
        t.wait()
    owned.wait()
    keptk.wait()
    keptv.wait()
    kept.wait()
    over(lambda i: vback(i).wait())
    over(lambda i: kback(i).wait())
    over(lambda i: gcopy(i).wait())


def main(owner, place, frames, freq, keys, values, gk, gv, q, do, n):
    tok = keys.shape[0]
    blocks = tok // BLOCK
    g = gk.shape[0]
    shard = g // n
    near = g + BLOCK
    smem, vmem, any_ = (pl.BlockSpec(memory_space=m) for m in (pltpu.SMEM, pltpu.VMEM, pl.ANY))
    dma = lambda k: pltpu.SemaphoreType.DMA((k,))
    slots = pltpu.VMEM((n * SLOTS, BLOCK, D), BF16)
    mine = pltpu.VMEM((blocks, BLOCK, D), BF16)
    ends = pltpu.VMEM((blocks * FAR, BLOCK, D), BF16)
    return pl.pallas_call(
        functools.partial(main_kernel, n),
        in_specs=[smem] * 2 + [vmem] * 6 + [any_] * 2,
        out_specs=[any_] * 7 + [smem],
        out_shape=[
            jax.ShapeDtypeStruct((tok, HEADS * D), F32),
            jax.ShapeDtypeStruct((blocks, BLOCK, 2 * D), F32),
            jax.ShapeDtypeStruct((n * SLOTS, BLOCK, D), BF16),
            jax.ShapeDtypeStruct((n * SLOTS, BLOCK, D), BF16),
            jax.ShapeDtypeStruct((n, shard, 2 * D), BF16),
            jax.ShapeDtypeStruct((tok, D), F32),
            jax.ShapeDtypeStruct((tok, D), F32),
            jax.ShapeDtypeStruct((n * SLOTS,), jnp.int32),
        ],
        scratch_shapes=[
            pltpu.VMEM((tok, D), F32),
            pltpu.VMEM((tok, D), F32),
            mine, mine, slots, slots, slots, slots, ends, ends, slots, slots,
            pltpu.VMEM((near + FAR * BLOCK, D), BF16),
            pltpu.VMEM((near, D), BF16),
            pltpu.VMEM((blocks, BLOCK, HEADS * D), BF16),
            pltpu.VMEM((blocks, BLOCK, HEADS * D), BF16),
            pltpu.VMEM((blocks, ROWS, D), BF16),
            pltpu.VMEM((blocks, ROWS, D), BF16),
            pltpu.VMEM((blocks, near + FAR * BLOCK, ROWS), BF16),
            pltpu.VMEM((near, ROWS), BF16),
            pltpu.VMEM((blocks, FAR * BLOCK, ROWS), F32),
            pltpu.VMEM((blocks, BLOCK, HEADS * D), F32),
            pltpu.VMEM((blocks, BLOCK, 2 * D), F32),
            pltpu.VMEM((blocks, 8, ROWS), F32),
            pltpu.VMEM((g, 2 * D), F32),
            pltpu.VMEM((n, shard, 2 * D), BF16),
            pltpu.VMEM((n, shard, 2 * D), BF16),
            pltpu.VMEM((shard, 2 * D), BF16),
            pltpu.SMEM((n * SLOTS,), jnp.int32),
            pltpu.SMEM((blocks * FAR,), jnp.int32),
            dma(blocks), dma(blocks), dma(blocks),
        ] + [dma(n)] * 12 + [dma(6)],
        compiler_params=pltpu.CompilerParams(
            collective_id=0, has_side_effects=True, vmem_limit_bytes=58 << 20
        ),
        name="main",
    )(owner, place, frames, freq, keys, values, gk, gv, q, do)


def final_kernel(
    index_ref, dq_hbm, dkv_hbm, backk_hbm, backv_hbm, glob_hbm, c_hbm, s_hbm,
    qg_hbm, kg_ref, vg_ref, gk_ref, gv_ref,
    acc, backk, backv, glob, c, s, held, isem, osem, sem,
):
    blocks = acc.shape[0]
    n, shard, _ = glob.shape
    total = backk.shape[0]
    tok = blocks * BLOCK
    pieces = isem.shape[0]
    step = tok // pieces
    loads = [
        pltpu.make_async_copy(src, dst, sem.at[i])
        for i, (src, dst) in enumerate(
            [(dkv_hbm, acc), (backk_hbm, backk), (backv_hbm, backv),
             (c_hbm, c), (s_hbm, s), (glob_hbm, glob)]
        )
    ]
    parts = [pl.ds(i * step, step) for i in range(pieces)]
    ins = [pltpu.make_async_copy(dq_hbm.at[r], held.at[r], isem.at[i]) for i, r in enumerate(parts)]
    outs = [pltpu.make_async_copy(held.at[r], qg_hbm.at[r], osem.at[i]) for i, r in enumerate(parts)]
    for m in loads + ins:
        m.start()
    for m in loads[:3]:
        m.wait()

    def add(i, carry):
        at = index_ref[i]

        @pl.when(at >= 0)
        def _():
            acc[at, :, :D] += backk[i].astype(F32)
            acc[at, :, D:] += backv[i].astype(F32)

        return carry

    lax.fori_loop(0, total // 2, add, 0)
    for i, m in enumerate(ins):
        m.wait()
        outs[i].start()
    lax.fori_loop(total // 2, total, add, 0)
    for m in loads[3:]:
        m.wait()
    for b in range(blocks):
        r = slice(b * BLOCK, (b + 1) * BLOCK)
        kg_ref[r] = unrot(acc[b, :, :D], c[r], s[r])
        vg_ref[r] = acc[b, :, D:]
    for i in range(n):
        gk_ref[i * shard : (i + 1) * shard] = glob[i, :, :D].astype(F32)
        gv_ref[i * shard : (i + 1) * shard] = glob[i, :, D:].astype(F32)
    for m in outs:
        m.wait()


def final(index, dq, dkv, backk, backv, glob, c, s):
    blocks = dkv.shape[0]
    tok = blocks * BLOCK
    n, shard, _ = glob.shape
    smem, vmem, any_ = (pl.BlockSpec(memory_space=m) for m in (pltpu.SMEM, pltpu.VMEM, pl.ANY))
    return pl.pallas_call(
        final_kernel,
        in_specs=[smem] + [any_] * 7,
        out_specs=[any_] + [vmem] * 4,
        out_shape=[
            jax.ShapeDtypeStruct((tok, HEADS * D), F32),
            jax.ShapeDtypeStruct((tok, D), F32),
            jax.ShapeDtypeStruct((tok, D), F32),
            jax.ShapeDtypeStruct((n * shard, D), F32),
            jax.ShapeDtypeStruct((n * shard, D), F32),
        ],
        scratch_shapes=[
            pltpu.VMEM(dkv.shape, F32),
            pltpu.VMEM(backk.shape, BF16),
            pltpu.VMEM(backv.shape, BF16),
            pltpu.VMEM(glob.shape, BF16),
            pltpu.VMEM((tok, D), F32),
            pltpu.VMEM((tok, D), F32),
            pltpu.VMEM((tok, HEADS * D), F32),
            pltpu.SemaphoreType.DMA((8,)),
            pltpu.SemaphoreType.DMA((8,)),
            pltpu.SemaphoreType.DMA((6,)),
        ],
        compiler_params=pltpu.CompilerParams(vmem_limit_bytes=60 << 20),
        name="final",
    )(index, dq, dkv, backk, backv, glob, c, s)


def on_device(queries, keys, values, dout, glob_keys, glob_values, frames, far_owner, far_local):
    n = lax.axis_size("ctx")
    dq, dkv, backk, backv, glob, c, s, index = main(
        far_owner.T, far_local.T, frames.reshape(-1, LANES), jnp.asarray(frequencies()),
        keys, values, glob_keys, glob_values, queries, dout, n,
    )
    return tuple(final(index, dq, dkv, backk, backv, glob, c, s))


def solution(mesh):
    both = P(("grp", "ctx"), None)
    one = P("grp", None)
    return jax.shard_map(
        on_device,
        mesh=mesh,
        in_specs=(both, both, both, both, one, one, P(("grp", "ctx")), one, one),
        out_specs=(both, both, both, one, one),
        check_vma=False,
    )
```

```python
import functools
import math

import jax
import jax.numpy as jnp
import numpy as np
from jax import lax
from jax.experimental import pallas as pl
from jax.experimental.pallas import tpu as pltpu
from jax.sharding import PartitionSpec as P

F32, BF16 = jnp.float32, jnp.bfloat16
MESH = pl.DeviceIdType.MESH
BLOCK, FAR, SLOTS, D, HEADS = 64, 2, 2, 128, 8
ROWS = BLOCK * HEADS

rope_base = 1000000.0
yarn_factor = 4.0
orig_context = 32768.0
ramp_low = 1.0
ramp_high = 32.0

FACTOR = (0.1 * math.log(yarn_factor) + 1.0) ** 2 / math.sqrt(D)
FACTOR2 = FACTOR * math.log2(math.e)

LANES = 128

NT = (((1,), (1,)), ((), ()))
NN = (((1,), (0,)), ((), ()))
TN = (((0,), (0,)), ((), ()))


def dot(a, b, dims):
    return lax.dot_general(a, b, dims, preferred_element_type=F32)


def frequencies():
    index = np.arange(D // 2, dtype=np.float64)
    inverse = rope_base ** (-2.0 * index / D)
    ratios = orig_context * inverse / (2.0 * math.pi)
    ramp = np.clip((ratios - ramp_low) / (ramp_high - ramp_low), 0.0, 1.0)
    frequency = inverse * ((1.0 - ramp) / yarn_factor + ramp)
    return np.concatenate([frequency, frequency])[None, :].astype(np.float32)


def rot(x, c, s):
    return x * c + pltpu.roll(x, D // 2, 1) * s


def unrot(x, c, s):
    return x * c - pltpu.roll(x, D // 2, 1) * s


def send_plan(i, n):
    return 1 + lax.rem(i * 11, n - 1)


def main_kernel(
    n, owner_ref, place_ref, frame_ref, freq_ref, k_ref, v_ref, gk_ref, gv_ref, q_hbm, do_hbm,
    dq_hbm, dkv_hbm, backk_ref, backv_ref, glob_ref, c_hbm, s_hbm, index_ref,
    c_ref, s_ref,
    ownk, ownv, sendk, sendv, recvk, recvv, retk, retv, rsendk, rsendv,
    kset, vset, qin, din, qr, dor, dsb, pb, pfar, dqs, dkvs, stats, gacc, part, parts, gsum,
    entry, slot,
    qsem, dsem, osem, kfs, kfr, vfs, vfr, kbs, kbr, vbs, vbr, rs, rr, gs, gr, lsem,
):
    me = lax.axis_index("ctx")
    blocks = ownk.shape[0]
    g = gk_ref.shape[0]
    near = g + BLOCK
    shard = g // n
    barrier = pltpu.get_barrier_semaphore()

    def peer(i):
        return lax.rem(me + send_plan(i, n), n)

    def over(f, count=n - 1, start=0):
        def body(i, carry):
            f(i)
            return carry

        lax.fori_loop(start, count, body, 0)

    over(
        lambda i: pl.semaphore_signal(
            barrier, inc=1, device_id={"ctx": peer(i)}, device_id_type=MESH
        )
    )

    def rows(b):
        return pl.ds(pl.multiple_of(b * BLOCK, BLOCK), BLOCK)

    def qcopy(b):
        return pltpu.make_async_copy(q_hbm.at[rows(b)], qin.at[b], qsem.at[b])

    def dcopy(b):
        return pltpu.make_async_copy(do_hbm.at[rows(b)], din.at[b], dsem.at[b])

    def ocopy(b):
        return pltpu.make_async_copy(dqs.at[b], dq_hbm.at[rows(b)], osem.at[b])

    def fetch(b):
        qcopy(b).start()
        dcopy(b).start()

    over(fetch, blocks)

    half = blocks * BLOCK // 2
    low = lax.broadcasted_iota(jnp.int32, (LANES, LANES), 1) < D // 2
    for i in range(half // LANES):
        spread = [
            jnp.broadcast_to(frame_ref[j : j + 1].astype(F32), (LANES, LANES)).T
            for j in (i, i + half // LANES)
        ]
        angle = jnp.where(low, spread[0], spread[1]) * freq_ref[...]
        cosine, sine = jnp.cos(angle), jnp.sin(angle)
        cturn, sturn = pltpu.roll(cosine, D // 2, 1), pltpu.roll(sine, D // 2, 1)
        r0 = slice(i * LANES, (i + 1) * LANES)
        r1 = slice(half + i * LANES, half + (i + 1) * LANES)
        c_ref[r0] = jnp.where(low, cosine, cturn)
        s_ref[r0] = jnp.where(low, -sine, sturn)
        c_ref[r1] = jnp.where(low, cturn, cosine)
        s_ref[r1] = jnp.where(low, -sturn, sine)
    tables = [
        pltpu.make_async_copy(c_ref, c_hbm, lsem.at[4]),
        pltpu.make_async_copy(s_ref, s_hbm, lsem.at[5]),
    ]
    for t in tables:
        t.start()

    def turn(b):
        x = k_ref[rows(b)].astype(F32)
        ownk[b] = rot(x, c_ref[rows(b)], s_ref[rows(b)]).astype(BF16)
        ownv[b] = v_ref[rows(b)]

    over(turn, blocks)

    def find(row, wanted, value):
        first = second = jnp.int32(-1)
        for b in reversed(range(blocks)):
            for f in reversed(range(FAR)):
                hit = owner_ref[f, row * blocks + b] == wanted
                second = jnp.where(hit, first, second)
                first = jnp.where(hit, value(f, b), first)
        return first, second

    def listed(d):
        for j, x in enumerate(find(d, me, lambda f, b: place_ref[f, d * blocks + b])):
            index_ref[d * SLOTS + j] = x

    def pair(ref, i):
        return ref.at[pl.ds(pl.multiple_of(i * SLOTS, SLOTS), SLOTS)]

    def remote(src, dst, ssem, rsem, i):
        return pltpu.make_async_remote_copy(
            src, dst, ssem.at[i], rsem.at[i], device_id={"ctx": peer(i)}, device_id_type=MESH
        )

    def kcopy(i):
        return remote(pair(sendk, peer(i)), pair(recvk, me), kfs, kfr, i)

    def vcopy(i):
        return remote(pair(sendv, peer(i)), pair(recvv, me), vfs, vfr, i)

    def kback(i):
        return remote(pair(rsendk, peer(i)), pair(backk_ref, me), kbs, kbr, i)

    def vback(i):
        return remote(pair(rsendv, peer(i)), pair(backv_ref, me), vbs, vbr, i)

    def rcopy(i):
        return remote(part.at[peer(i)], parts.at[me], rs, rr, i)

    def gcopy(i):
        return remote(gsum, glob_ref.at[me], gs, gr, i)

    def lay(dst, src, to, table):
        for j in range(SLOTS):
            dst[to * SLOTS + j] = src[jnp.maximum(table[to * SLOTS + j], 0)]

    pl.semaphore_wait(barrier, n - 1)

    def give_k(i):
        listed(peer(i))
        lay(sendk, ownk, peer(i), index_ref)
        kcopy(i).start()

    def give_v(i):
        lay(sendv, ownv, peer(i), index_ref)
        vcopy(i).start()

    over(give_k)
    over(give_v)
    listed(me)
    lay(recvk, ownk, me, index_ref)
    lay(recvv, ownv, me, index_ref)

    def mine(o):
        for j, x in enumerate(find(me, o, lambda f, b: jnp.int32(b * FAR + f))):
            entry[o * SLOTS + j] = x

    over(mine, n)

    def seat(b):
        for f in range(FAR):
            o = owner_ref[f, me * blocks + b]
            later = entry[o * SLOTS] != b * FAR + f
            slot[b * FAR + f] = o * SLOTS + later.astype(jnp.int32)

    over(seat, blocks)

    kset[:g] = gk_ref[...]
    vset[:g] = gv_ref[...]
    width = 512

    def near_stats(b):
        qcopy(b).wait()
        dcopy(b).wait()
        kset[g:near] = ownk[b]
        vset[g:near] = ownv[b]
        c, s = c_ref[rows(b)], s_ref[rows(b)]
        for h in range(HEADS):
            at, cols = slice(h * BLOCK, (h + 1) * BLOCK), slice(h * D, (h + 1) * D)
            qr[b, at] = rot(qin[b, :, cols].astype(F32), c, s).astype(BF16)
            dor[b, at] = din[b, :, cols]
        for j in range(0, ROWS, width):
            at = slice(j, j + width)
            scores = dot(kset[:near], qr[b, at], NT)
            dp = dot(vset[:near], dor[b, at], NT)
            top = jnp.max(scores, axis=0, keepdims=True)
            e = jnp.exp2(scores * FACTOR2 - top * FACTOR2)
            stats[b, 0:1, at] = top
            stats[b, 1:2, at] = jnp.sum(e, axis=0, keepdims=True)
            stats[b, 2:3, at] = jnp.sum(e * dp, axis=0, keepdims=True)

    over(near_stats, blocks)

    over(lambda i: kcopy(i).wait_recv())

    def halves(x):
        return [x[f * BLOCK : (f + 1) * BLOCK] for f in range(FAR)]

    def far_values(b):
        fk = jnp.concatenate([recvk[slot[b * FAR + f]] for f in range(FAR)], axis=0)
        scores = dot(fk, qr[b], NT)
        top0 = stats[b, 0:1, :]
        top = jnp.maximum(jnp.max(scores, axis=0, keepdims=True), top0)
        shrink = jnp.exp2(top0 * FACTOR2 - top * FACTOR2)
        e = jnp.exp2(scores * FACTOR2 - top * FACTOR2)
        total = stats[b, 1:2, :] * shrink + jnp.sum(e, axis=0, keepdims=True)
        w = 1.0 / total
        p = e * w
        pfar[b] = p
        stats[b, 3:4, :] = top * FACTOR2 + jnp.log(total) * math.log2(math.e)
        stats[b, 4:5, :] = stats[b, 2:3, :] * shrink * w
        for f, x in enumerate(halves(dot(p.astype(BF16), dor[b], NN))):
            retv[b * FAR + f] = x.astype(BF16)

    over(far_values, blocks)

    def return_v(i):
        lay(rsendv, retv, peer(i), entry)
        vback(i).start()

    over(return_v)

    over(lambda i: vcopy(i).wait_recv())

    def far_keys(b):
        fv = jnp.concatenate([recvv[slot[b * FAR + f]] for f in range(FAR)], axis=0)
        dp = dot(fv, dor[b], NT)
        p = pfar[b]
        delta = stats[b, 4:5, :] + jnp.sum(p * dp, axis=0, keepdims=True)
        stats[b, 5:6, :] = delta
        ds = (p * (dp - delta)).astype(BF16)
        dsb[b, near:] = ds
        for f, x in enumerate(halves(dot(ds, qr[b], NN) * FACTOR)):
            retk[b * FAR + f] = x.astype(BF16)

    over(far_keys, blocks)

    def return_k(i):
        lay(rsendk, retk, peer(i), entry)
        kback(i).start()

    over(return_k, 24)
    lay(rsendk, retk, me, entry)
    lay(rsendv, retv, me, entry)
    keptk = pltpu.make_async_copy(pair(rsendk, me), pair(backk_ref, me), lsem.at[0])
    keptv = pltpu.make_async_copy(pair(rsendv, me), pair(backv_ref, me), lsem.at[1])
    keptk.start()
    keptv.start()

    gacc[...] = jnp.zeros_like(gacc)

    def near_pass(b):
        kset[g:near] = ownk[b]
        vset[g:near] = ownv[b]
        for j in range(0, ROWS, width):
            at = slice(j, j + width)
            scores = dot(kset[:near], qr[b, at], NT)
            dp = dot(vset[:near], dor[b, at], NT)
            p = jnp.exp2(scores * FACTOR2 - stats[b, 3:4, at])
            pb[:, at] = p.astype(BF16)
            dsb[b, :near, at] = (p * (dp - stats[b, 5:6, at])).astype(BF16)
        dk = dot(dsb[b, :near], qr[b], NN) * FACTOR
        dv = dot(pb[...], dor[b], NN)
        gacc[:, :D] += dk[:g]
        gacc[:, D:] += dv[:g]
        dkvs[b, :, :D] = dk[g:]
        dkvs[b, :, D:] = dv[g:]

    over(near_pass, blocks)
    for i in range(n):
        part[i] = gacc[i * shard : (i + 1) * shard].astype(BF16)
    over(lambda i: rcopy(i).start())
    over(return_k, n - 1, 24)
    parts[me] = part[me]
    owned = pltpu.make_async_copy(dkvs, dkv_hbm, lsem.at[2])
    owned.start()

    def query_pass(b):
        kset[g:near] = ownk[b]
        for f in range(FAR):
            kset[near + f * BLOCK : near + (f + 1) * BLOCK] = recvk[slot[b * FAR + f]]
        dq = dot(dsb[b], kset[...], TN) * FACTOR
        c, s = c_ref[rows(b)], s_ref[rows(b)]
        for h in range(HEADS):
            dqs[b, :, h * D : (h + 1) * D] = unrot(dq[h * BLOCK : (h + 1) * BLOCK], c, s)
        ocopy(b).start()

    over(query_pass, 10)

    over(lambda i: rcopy(i).wait_recv())
    gsum[...] = jnp.sum(parts[...].astype(F32), axis=0).astype(BF16)
    over(lambda i: gcopy(i).start())
    kept = pltpu.make_async_copy(gsum, glob_ref.at[me], lsem.at[3])
    kept.start()
    over(query_pass, blocks, 10)
    over(lambda i: kcopy(i).wait_send())
    over(lambda i: vcopy(i).wait_send())
    over(lambda i: rcopy(i).wait_send())
    over(lambda b: ocopy(b).wait(), blocks)
    for t in tables:
        t.wait()
    owned.wait()
    keptk.wait()
    keptv.wait()
    kept.wait()
    over(lambda i: vback(i).wait())
    over(lambda i: kback(i).wait())
    over(lambda i: gcopy(i).wait())


def main(owner, place, frames, freq, keys, values, gk, gv, q, do, n):
    tok = keys.shape[0]
    blocks = tok // BLOCK
    g = gk.shape[0]
    shard = g // n
    near = g + BLOCK
    smem, vmem, any_ = (pl.BlockSpec(memory_space=m) for m in (pltpu.SMEM, pltpu.VMEM, pl.ANY))
    dma = lambda k: pltpu.SemaphoreType.DMA((k,))
    slots = pltpu.VMEM((n * SLOTS, BLOCK, D), BF16)
    mine = pltpu.VMEM((blocks, BLOCK, D), BF16)
    ends = pltpu.VMEM((blocks * FAR, BLOCK, D), BF16)
    return pl.pallas_call(
        functools.partial(main_kernel, n),
        in_specs=[smem] * 2 + [vmem] * 6 + [any_] * 2,
        out_specs=[any_] * 7 + [smem],
        out_shape=[
            jax.ShapeDtypeStruct((tok, HEADS * D), F32),
            jax.ShapeDtypeStruct((blocks, BLOCK, 2 * D), F32),
            jax.ShapeDtypeStruct((n * SLOTS, BLOCK, D), BF16),
            jax.ShapeDtypeStruct((n * SLOTS, BLOCK, D), BF16),
            jax.ShapeDtypeStruct((n, shard, 2 * D), BF16),
            jax.ShapeDtypeStruct((tok, D), F32),
            jax.ShapeDtypeStruct((tok, D), F32),
            jax.ShapeDtypeStruct((n * SLOTS,), jnp.int32),
        ],
        scratch_shapes=[
            pltpu.VMEM((tok, D), F32),
            pltpu.VMEM((tok, D), F32),
            mine, mine, slots, slots, slots, slots, ends, ends, slots, slots,
            pltpu.VMEM((near + FAR * BLOCK, D), BF16),
            pltpu.VMEM((near, D), BF16),
            pltpu.VMEM((blocks, BLOCK, HEADS * D), BF16),
            pltpu.VMEM((blocks, BLOCK, HEADS * D), BF16),
            pltpu.VMEM((blocks, ROWS, D), BF16),
            pltpu.VMEM((blocks, ROWS, D), BF16),
            pltpu.VMEM((blocks, near + FAR * BLOCK, ROWS), BF16),
            pltpu.VMEM((near, ROWS), BF16),
            pltpu.VMEM((blocks, FAR * BLOCK, ROWS), F32),
            pltpu.VMEM((blocks, BLOCK, HEADS * D), F32),
            pltpu.VMEM((blocks, BLOCK, 2 * D), F32),
            pltpu.VMEM((blocks, 8, ROWS), F32),
            pltpu.VMEM((g, 2 * D), F32),
            pltpu.VMEM((n, shard, 2 * D), BF16),
            pltpu.VMEM((n, shard, 2 * D), BF16),
            pltpu.VMEM((shard, 2 * D), BF16),
            pltpu.SMEM((n * SLOTS,), jnp.int32),
            pltpu.SMEM((blocks * FAR,), jnp.int32),
            dma(blocks), dma(blocks), dma(blocks),
        ] + [dma(n)] * 12 + [dma(6)],
        compiler_params=pltpu.CompilerParams(
            collective_id=0, has_side_effects=True, vmem_limit_bytes=58 << 20
        ),
        name="main",
    )(owner, place, frames, freq, keys, values, gk, gv, q, do)


def final_kernel(
    index_ref, dq_hbm, dkv_hbm, backk_hbm, backv_hbm, glob_hbm, c_hbm, s_hbm,
    qg_hbm, kg_ref, vg_ref, gk_ref, gv_ref,
    acc, backk, backv, glob, c, s, held, isem, osem, sem,
):
    blocks = acc.shape[0]
    n, shard, _ = glob.shape
    total = backk.shape[0]
    tok = blocks * BLOCK
    pieces = isem.shape[0]
    step = tok // pieces
    loads = [
        pltpu.make_async_copy(src, dst, sem.at[i])
        for i, (src, dst) in enumerate(
            [(dkv_hbm, acc), (backk_hbm, backk), (backv_hbm, backv),
             (c_hbm, c), (s_hbm, s), (glob_hbm, glob)]
        )
    ]
    parts = [pl.ds(i * step, step) for i in range(pieces)]
    ins = [pltpu.make_async_copy(dq_hbm.at[r], held.at[r], isem.at[i]) for i, r in enumerate(parts)]
    outs = [pltpu.make_async_copy(held.at[r], qg_hbm.at[r], osem.at[i]) for i, r in enumerate(parts)]
    for m in loads + ins:
        m.start()
    for m in loads[:3]:
        m.wait()

    def add(i, carry):
        at = index_ref[i]

        @pl.when(at >= 0)
        def _():
            acc[at, :, :D] += backk[i].astype(F32)
            acc[at, :, D:] += backv[i].astype(F32)

        return carry

    lax.fori_loop(0, total // 2, add, 0)
    for i, m in enumerate(ins):
        m.wait()
        outs[i].start()
    lax.fori_loop(total // 2, total, add, 0)
    for m in loads[3:]:
        m.wait()
    for b in range(blocks):
        r = slice(b * BLOCK, (b + 1) * BLOCK)
        kg_ref[r] = unrot(acc[b, :, :D], c[r], s[r])
        vg_ref[r] = acc[b, :, D:]
    for i in range(n):
        gk_ref[i * shard : (i + 1) * shard] = glob[i, :, :D].astype(F32)
        gv_ref[i * shard : (i + 1) * shard] = glob[i, :, D:].astype(F32)
    for m in outs:
        m.wait()


def final(index, dq, dkv, backk, backv, glob, c, s):
    blocks = dkv.shape[0]
    tok = blocks * BLOCK
    n, shard, _ = glob.shape
    smem, vmem, any_ = (pl.BlockSpec(memory_space=m) for m in (pltpu.SMEM, pltpu.VMEM, pl.ANY))
    return pl.pallas_call(
        final_kernel,
        in_specs=[smem] + [any_] * 7,
        out_specs=[any_] + [vmem] * 4,
        out_shape=[
            jax.ShapeDtypeStruct((tok, HEADS * D), F32),
            jax.ShapeDtypeStruct((tok, D), F32),
            jax.ShapeDtypeStruct((tok, D), F32),
            jax.ShapeDtypeStruct((n * shard, D), F32),
            jax.ShapeDtypeStruct((n * shard, D), F32),
        ],
        scratch_shapes=[
            pltpu.VMEM(dkv.shape, F32),
            pltpu.VMEM(backk.shape, BF16),
            pltpu.VMEM(backv.shape, BF16),
            pltpu.VMEM(glob.shape, BF16),
            pltpu.VMEM((tok, D), F32),
            pltpu.VMEM((tok, D), F32),
            pltpu.VMEM((tok, HEADS * D), F32),
            pltpu.SemaphoreType.DMA((8,)),
            pltpu.SemaphoreType.DMA((8,)),
            pltpu.SemaphoreType.DMA((6,)),
        ],
        compiler_params=pltpu.CompilerParams(vmem_limit_bytes=60 << 20),
        name="final",
    )(index, dq, dkv, backk, backv, glob, c, s)


def on_device(queries, keys, values, dout, glob_keys, glob_values, frames, far_owner, far_local):
    n = lax.axis_size("ctx")
    dq, dkv, backk, backv, glob, c, s, index = main(
        far_owner.T, far_local.T, frames.reshape(-1, LANES), jnp.asarray(frequencies()),
        keys, values, glob_keys, glob_values, queries, dout, n,
    )
    return tuple(final(index, dq, dkv, backk, backv, glob, c, s))


def solution(mesh):
    both = P(("grp", "ctx"), None)
    one = P("grp", None)
    return jax.shard_map(
        on_device,
        mesh=mesh,
        in_specs=(both, both, both, both, one, one, P(("grp", "ctx")), one, one),
        out_specs=(both, both, both, one, one),
        check_vma=False,
    )
```

```python
import functools
import math

import jax
import jax.numpy as jnp
import numpy as np
from jax import lax
from jax.experimental import pallas as pl
from jax.experimental.pallas import tpu as pltpu
from jax.sharding import PartitionSpec as P

F32, BF16 = jnp.float32, jnp.bfloat16
MESH = pl.DeviceIdType.MESH
BLOCK, FAR, SLOTS, D, HEADS = 64, 2, 2, 128, 8
ROWS = BLOCK * HEADS

rope_base = 1000000.0
yarn_factor = 4.0
orig_context = 32768.0
ramp_low = 1.0
ramp_high = 32.0

FACTOR = (0.1 * math.log(yarn_factor) + 1.0) ** 2 / math.sqrt(D)
FACTOR2 = FACTOR * math.log2(math.e)

LANES = 128

NT = (((1,), (1,)), ((), ()))
NN = (((1,), (0,)), ((), ()))
TN = (((0,), (0,)), ((), ()))


def dot(a, b, dims):
    return lax.dot_general(a, b, dims, preferred_element_type=F32)


def frequencies():
    index = np.arange(D // 2, dtype=np.float64)
    inverse = rope_base ** (-2.0 * index / D)
    ratios = orig_context * inverse / (2.0 * math.pi)
    ramp = np.clip((ratios - ramp_low) / (ramp_high - ramp_low), 0.0, 1.0)
    frequency = inverse * ((1.0 - ramp) / yarn_factor + ramp)
    return np.concatenate([frequency, frequency])[None, :].astype(np.float32)


def rot(x, c, s):
    return x * c + pltpu.roll(x, D // 2, 1) * s


def unrot(x, c, s):
    return x * c - pltpu.roll(x, D // 2, 1) * s


def send_plan(i, n):
    return 1 + lax.rem(i * 11, n - 1)


def main_kernel(
    n, owner_ref, place_ref, frame_ref, freq_ref, k_hbm, v_hbm, gk_hbm, gv_hbm, q_hbm, do_hbm,
    dq_hbm, dkv_hbm, backk_ref, backv_ref, glob_ref, c_hbm, s_hbm, index_ref,
    c_ref, s_ref, k_ref,
    ownk, ownv, sendk, sendv, recvk, recvv, retk, retv, rsendk, rsendv,
    kset, vset, qin, din, qr, dor, dsb, pb, pfar, dqs, dkvs, stats, gacc, part, parts, gsum,
    entry, slot,
    qsem, dsem, osem, kfs, kfr, vfs, vfr, kbs, kbr, vbs, vbr, rs, rr, gs, gr, lsem,
):
    me = lax.axis_index("ctx")
    blocks = ownk.shape[0]
    g = gk_hbm.shape[0]
    near = g + BLOCK
    shard = g // n
    barrier = pltpu.get_barrier_semaphore()

    def peer(i):
        return lax.rem(me + send_plan(i, n), n)

    def over(f, count=n - 1, start=0):
        def body(i, carry):
            f(i)
            return carry

        lax.fori_loop(start, count, body, 0)

    over(
        lambda i: pl.semaphore_signal(
            barrier, inc=1, device_id={"ctx": peer(i)}, device_id_type=MESH
        )
    )

    def rows(b):
        return pl.ds(pl.multiple_of(b * BLOCK, BLOCK), BLOCK)

    def qcopy(b):
        return pltpu.make_async_copy(q_hbm.at[rows(b)], qin.at[b], qsem.at[b])

    def dcopy(b):
        return pltpu.make_async_copy(do_hbm.at[rows(b)], din.at[b], dsem.at[b])

    def ocopy(b):
        return pltpu.make_async_copy(dqs.at[b], dq_hbm.at[rows(b)], osem.at[b])

    def fetch(b):
        qcopy(b).start()
        dcopy(b).start()

    brought = [
        pltpu.make_async_copy(src, dst, lsem.at[6 + i])
        for i, (src, dst) in enumerate(
            [(k_hbm, k_ref), (v_hbm, ownv),
             (gk_hbm, kset.at[pl.ds(0, g)]), (gv_hbm, vset.at[pl.ds(0, g)])]
        )
    ]
    for x in brought:
        x.start()
    over(fetch, blocks)

    half = blocks * BLOCK // 2
    low = lax.broadcasted_iota(jnp.int32, (LANES, LANES), 1) < D // 2
    for i in range(half // LANES):
        spread = [
            jnp.broadcast_to(frame_ref[j : j + 1].astype(F32), (LANES, LANES)).T
            for j in (i, i + half // LANES)
        ]
        angle = jnp.where(low, spread[0], spread[1]) * freq_ref[...]
        cosine, sine = jnp.cos(angle), jnp.sin(angle)
        cturn, sturn = pltpu.roll(cosine, D // 2, 1), pltpu.roll(sine, D // 2, 1)
        r0 = slice(i * LANES, (i + 1) * LANES)
        r1 = slice(half + i * LANES, half + (i + 1) * LANES)
        c_ref[r0] = jnp.where(low, cosine, cturn)
        s_ref[r0] = jnp.where(low, -sine, sturn)
        c_ref[r1] = jnp.where(low, cturn, cosine)
        s_ref[r1] = jnp.where(low, -sturn, sine)
    tables = [
        pltpu.make_async_copy(c_ref, c_hbm, lsem.at[4]),
        pltpu.make_async_copy(s_ref, s_hbm, lsem.at[5]),
    ]
    for t in tables:
        t.start()

    def turn(b):
        x = k_ref[rows(b)].astype(F32)
        ownk[b] = rot(x, c_ref[rows(b)], s_ref[rows(b)]).astype(BF16)

    brought[0].wait()
    over(turn, blocks)

    def find(row, wanted, value):
        first = second = jnp.int32(-1)
        for b in reversed(range(blocks)):
            for f in reversed(range(FAR)):
                hit = owner_ref[f, row * blocks + b] == wanted
                second = jnp.where(hit, first, second)
                first = jnp.where(hit, value(f, b), first)
        return first, second

    def listed(d):
        for j, x in enumerate(find(d, me, lambda f, b: place_ref[f, d * blocks + b])):
            index_ref[d * SLOTS + j] = x

    def pair(ref, i):
        return ref.at[pl.ds(pl.multiple_of(i * SLOTS, SLOTS), SLOTS)]

    def remote(src, dst, ssem, rsem, i):
        return pltpu.make_async_remote_copy(
            src, dst, ssem.at[i], rsem.at[i], device_id={"ctx": peer(i)}, device_id_type=MESH
        )

    def kcopy(i):
        return remote(pair(sendk, peer(i)), pair(recvk, me), kfs, kfr, i)

    def vcopy(i):
        return remote(pair(sendv, peer(i)), pair(recvv, me), vfs, vfr, i)

    def kback(i):
        return remote(pair(rsendk, peer(i)), pair(backk_ref, me), kbs, kbr, i)

    def vback(i):
        return remote(pair(rsendv, peer(i)), pair(backv_ref, me), vbs, vbr, i)

    def rcopy(i):
        return remote(part.at[peer(i)], parts.at[me], rs, rr, i)

    def gcopy(i):
        return remote(gsum, glob_ref.at[me], gs, gr, i)

    def lay(dst, src, to, table):
        for j in range(SLOTS):
            dst[to * SLOTS + j] = src[jnp.maximum(table[to * SLOTS + j], 0)]

    pl.semaphore_wait(barrier, n - 1)

    def give_k(i):
        listed(peer(i))
        lay(sendk, ownk, peer(i), index_ref)
        kcopy(i).start()

    def give_v(i):
        lay(sendv, ownv, peer(i), index_ref)
        vcopy(i).start()

    over(give_k)
    brought[1].wait()
    over(give_v)
    listed(me)
    lay(recvk, ownk, me, index_ref)
    lay(recvv, ownv, me, index_ref)

    def mine(o):
        for j, x in enumerate(find(me, o, lambda f, b: jnp.int32(b * FAR + f))):
            entry[o * SLOTS + j] = x

    over(mine, n)

    def seat(b):
        for f in range(FAR):
            o = owner_ref[f, me * blocks + b]
            later = entry[o * SLOTS] != b * FAR + f
            slot[b * FAR + f] = o * SLOTS + later.astype(jnp.int32)

    over(seat, blocks)

    brought[2].wait()
    brought[3].wait()
    width = 512

    def near_stats(b):
        qcopy(b).wait()
        dcopy(b).wait()
        kset[g:near] = ownk[b]
        vset[g:near] = ownv[b]
        c, s = c_ref[rows(b)], s_ref[rows(b)]
        for h in range(HEADS):
            at, cols = slice(h * BLOCK, (h + 1) * BLOCK), slice(h * D, (h + 1) * D)
            qr[b, at] = rot(qin[b, :, cols].astype(F32), c, s).astype(BF16)
            dor[b, at] = din[b, :, cols]
        for j in range(0, ROWS, width):
            at = slice(j, j + width)
            scores = dot(kset[:near], qr[b, at], NT)
            dp = dot(vset[:near], dor[b, at], NT)
            top = jnp.max(scores, axis=0, keepdims=True)
            e = jnp.exp2(scores * FACTOR2 - top * FACTOR2)
            stats[b, 0:1, at] = top
            stats[b, 1:2, at] = jnp.sum(e, axis=0, keepdims=True)
            stats[b, 2:3, at] = jnp.sum(e * dp, axis=0, keepdims=True)

    over(near_stats, blocks)

    over(lambda i: kcopy(i).wait_recv())

    def halves(x):
        return [x[f * BLOCK : (f + 1) * BLOCK] for f in range(FAR)]

    def far_values(b):
        fk = jnp.concatenate([recvk[slot[b * FAR + f]] for f in range(FAR)], axis=0)
        scores = dot(fk, qr[b], NT)
        top0 = stats[b, 0:1, :]
        top = jnp.maximum(jnp.max(scores, axis=0, keepdims=True), top0)
        shrink = jnp.exp2(top0 * FACTOR2 - top * FACTOR2)
        e = jnp.exp2(scores * FACTOR2 - top * FACTOR2)
        total = stats[b, 1:2, :] * shrink + jnp.sum(e, axis=0, keepdims=True)
        w = 1.0 / total
        p = e * w
        pfar[b] = p
        stats[b, 3:4, :] = top * FACTOR2 + jnp.log(total) * math.log2(math.e)
        stats[b, 4:5, :] = stats[b, 2:3, :] * shrink * w
        for f, x in enumerate(halves(dot(p.astype(BF16), dor[b], NN))):
            retv[b * FAR + f] = x.astype(BF16)

    over(far_values, blocks)

    def return_v(i):
        lay(rsendv, retv, peer(i), entry)
        vback(i).start()

    over(return_v)

    over(lambda i: vcopy(i).wait_recv())

    def far_keys(b):
        fv = jnp.concatenate([recvv[slot[b * FAR + f]] for f in range(FAR)], axis=0)
        dp = dot(fv, dor[b], NT)
        p = pfar[b]
        delta = stats[b, 4:5, :] + jnp.sum(p * dp, axis=0, keepdims=True)
        stats[b, 5:6, :] = delta
        ds = (p * (dp - delta)).astype(BF16)
        dsb[b, near:] = ds
        for f, x in enumerate(halves(dot(ds, qr[b], NN) * FACTOR)):
            retk[b * FAR + f] = x.astype(BF16)

    over(far_keys, blocks)

    def return_k(i):
        lay(rsendk, retk, peer(i), entry)
        kback(i).start()

    over(return_k, 24)
    lay(rsendk, retk, me, entry)
    lay(rsendv, retv, me, entry)
    keptk = pltpu.make_async_copy(pair(rsendk, me), pair(backk_ref, me), lsem.at[0])
    keptv = pltpu.make_async_copy(pair(rsendv, me), pair(backv_ref, me), lsem.at[1])
    keptk.start()
    keptv.start()

    gacc[...] = jnp.zeros_like(gacc)

    def near_pass(b):
        kset[g:near] = ownk[b]
        vset[g:near] = ownv[b]
        for j in range(0, ROWS, width):
            at = slice(j, j + width)
            scores = dot(kset[:near], qr[b, at], NT)
            dp = dot(vset[:near], dor[b, at], NT)
            p = jnp.exp2(scores * FACTOR2 - stats[b, 3:4, at])
            pb[:, at] = p.astype(BF16)
            dsb[b, :near, at] = (p * (dp - stats[b, 5:6, at])).astype(BF16)
        dk = dot(dsb[b, :near], qr[b], NN) * FACTOR
        dv = dot(pb[...], dor[b], NN)
        gacc[:, :D] += dk[:g]
        gacc[:, D:] += dv[:g]
        dkvs[b, :, :D] = dk[g:]
        dkvs[b, :, D:] = dv[g:]

    over(near_pass, blocks)
    for i in range(n):
        part[i] = gacc[i * shard : (i + 1) * shard].astype(BF16)
    over(lambda i: rcopy(i).start())
    over(return_k, n - 1, 24)
    parts[me] = part[me]
    owned = pltpu.make_async_copy(dkvs, dkv_hbm, lsem.at[2])
    owned.start()

    def query_pass(b):
        kset[g:near] = ownk[b]
        for f in range(FAR):
            kset[near + f * BLOCK : near + (f + 1) * BLOCK] = recvk[slot[b * FAR + f]]
        dq = dot(dsb[b], kset[...], TN) * FACTOR
        c, s = c_ref[rows(b)], s_ref[rows(b)]
        for h in range(HEADS):
            dqs[b, :, h * D : (h + 1) * D] = unrot(dq[h * BLOCK : (h + 1) * BLOCK], c, s)
        ocopy(b).start()

    over(query_pass, 10)

    over(lambda i: rcopy(i).wait_recv())
    gsum[...] = jnp.sum(parts[...].astype(F32), axis=0).astype(BF16)
    over(lambda i: gcopy(i).start())
    kept = pltpu.make_async_copy(gsum, glob_ref.at[me], lsem.at[3])
    kept.start()
    over(query_pass, blocks, 10)
    over(lambda i: kcopy(i).wait_send())
    over(lambda i: vcopy(i).wait_send())
    over(lambda i: rcopy(i).wait_send())
    over(lambda b: ocopy(b).wait(), blocks)
    for t in tables:
        t.wait()
    owned.wait()
    keptk.wait()
    keptv.wait()
    kept.wait()
    over(lambda i: vback(i).wait())
    over(lambda i: kback(i).wait())
    over(lambda i: gcopy(i).wait())


def main(owner, place, frames, freq, keys, values, gk, gv, q, do, n):
    tok = keys.shape[0]
    blocks = tok // BLOCK
    g = gk.shape[0]
    shard = g // n
    near = g + BLOCK
    smem, vmem, any_ = (pl.BlockSpec(memory_space=m) for m in (pltpu.SMEM, pltpu.VMEM, pl.ANY))
    dma = lambda k: pltpu.SemaphoreType.DMA((k,))
    slots = pltpu.VMEM((n * SLOTS, BLOCK, D), BF16)
    mine = pltpu.VMEM((blocks, BLOCK, D), BF16)
    ends = pltpu.VMEM((blocks * FAR, BLOCK, D), BF16)
    return pl.pallas_call(
        functools.partial(main_kernel, n),
        in_specs=[smem] * 2 + [vmem] * 2 + [any_] * 6,
        out_specs=[any_] * 7 + [smem],
        out_shape=[
            jax.ShapeDtypeStruct((tok, HEADS * D), F32),
            jax.ShapeDtypeStruct((blocks, BLOCK, 2 * D), F32),
            jax.ShapeDtypeStruct((n * SLOTS, BLOCK, D), BF16),
            jax.ShapeDtypeStruct((n * SLOTS, BLOCK, D), BF16),
            jax.ShapeDtypeStruct((n, shard, 2 * D), BF16),
            jax.ShapeDtypeStruct((tok, D), F32),
            jax.ShapeDtypeStruct((tok, D), F32),
            jax.ShapeDtypeStruct((n * SLOTS,), jnp.int32),
        ],
        scratch_shapes=[
            pltpu.VMEM((tok, D), F32),
            pltpu.VMEM((tok, D), F32),
            pltpu.VMEM((tok, D), BF16),
            mine, mine, slots, slots, slots, slots, ends, ends, slots, slots,
            pltpu.VMEM((near + FAR * BLOCK, D), BF16),
            pltpu.VMEM((near, D), BF16),
            pltpu.VMEM((blocks, BLOCK, HEADS * D), BF16),
            pltpu.VMEM((blocks, BLOCK, HEADS * D), BF16),
            pltpu.VMEM((blocks, ROWS, D), BF16),
            pltpu.VMEM((blocks, ROWS, D), BF16),
            pltpu.VMEM((blocks, near + FAR * BLOCK, ROWS), BF16),
            pltpu.VMEM((near, ROWS), BF16),
            pltpu.VMEM((blocks, FAR * BLOCK, ROWS), F32),
            pltpu.VMEM((blocks, BLOCK, HEADS * D), F32),
            pltpu.VMEM((blocks, BLOCK, 2 * D), F32),
            pltpu.VMEM((blocks, 8, ROWS), F32),
            pltpu.VMEM((g, 2 * D), F32),
            pltpu.VMEM((n, shard, 2 * D), BF16),
            pltpu.VMEM((n, shard, 2 * D), BF16),
            pltpu.VMEM((shard, 2 * D), BF16),
            pltpu.SMEM((n * SLOTS,), jnp.int32),
            pltpu.SMEM((blocks * FAR,), jnp.int32),
            dma(blocks), dma(blocks), dma(blocks),
        ] + [dma(n)] * 12 + [dma(10)],
        compiler_params=pltpu.CompilerParams(
            collective_id=0, has_side_effects=True, vmem_limit_bytes=58 << 20
        ),
        name="main",
    )(owner, place, frames, freq, keys, values, gk, gv, q, do)


def final_kernel(
    index_ref, dq_hbm, dkv_hbm, backk_hbm, backv_hbm, glob_hbm, c_hbm, s_hbm,
    qg_hbm, kg_hbm, vg_hbm, gk_hbm, gv_hbm,
    kg_ref, vg_ref, gk_ref, gv_ref, acc, backk, backv, glob, c, s, held, isem, osem, sem,
):
    blocks = acc.shape[0]
    n, shard, _ = glob.shape
    total = backk.shape[0]
    tok = blocks * BLOCK
    pieces = isem.shape[0]
    step = tok // pieces
    loads = [
        pltpu.make_async_copy(src, dst, sem.at[i])
        for i, (src, dst) in enumerate(
            [(dkv_hbm, acc), (backk_hbm, backk), (backv_hbm, backv),
             (c_hbm, c), (s_hbm, s), (glob_hbm, glob)]
        )
    ]
    parts = [pl.ds(i * step, step) for i in range(pieces)]
    ins = [pltpu.make_async_copy(dq_hbm.at[r], held.at[r], isem.at[i]) for i, r in enumerate(parts)]
    outs = [pltpu.make_async_copy(held.at[r], qg_hbm.at[r], osem.at[i]) for i, r in enumerate(parts)]
    for m in loads + ins:
        m.start()
    stores = [
        pltpu.make_async_copy(src, dst, sem.at[6 + i])
        for i, (src, dst) in enumerate(
            [(gk_ref, gk_hbm), (gv_ref, gv_hbm), (kg_ref, kg_hbm), (vg_ref, vg_hbm)]
        )
    ]
    for m in loads[:3]:
        m.wait()

    def add(i, carry):
        at = index_ref[i]

        @pl.when(at >= 0)
        def _():
            acc[at, :, :D] += backk[i].astype(F32)
            acc[at, :, D:] += backv[i].astype(F32)

        return carry

    lax.fori_loop(0, total // 2, add, 0, unroll=4)
    for i, m in enumerate(ins):
        m.wait()
        outs[i].start()
    lax.fori_loop(total // 2, total, add, 0, unroll=4)
    for m in loads[3:]:
        m.wait()
    for b in range(blocks):
        r = slice(b * BLOCK, (b + 1) * BLOCK)
        kg_ref[r] = unrot(acc[b, :, :D], c[r], s[r])
        vg_ref[r] = acc[b, :, D:]
    stores[2].start()
    stores[3].start()
    for i in range(n):
        gk_ref[i * shard : (i + 1) * shard] = glob[i, :, :D].astype(F32)
        gv_ref[i * shard : (i + 1) * shard] = glob[i, :, D:].astype(F32)
    stores[0].start()
    stores[1].start()
    for m in outs + stores:
        m.wait()


def final(index, dq, dkv, backk, backv, glob, c, s):
    blocks = dkv.shape[0]
    tok = blocks * BLOCK
    n, shard, _ = glob.shape
    smem, vmem, any_ = (pl.BlockSpec(memory_space=m) for m in (pltpu.SMEM, pltpu.VMEM, pl.ANY))
    return pl.pallas_call(
        final_kernel,
        in_specs=[smem] + [any_] * 7,
        out_specs=[any_] * 5,
        out_shape=[
            jax.ShapeDtypeStruct((tok, HEADS * D), F32),
            jax.ShapeDtypeStruct((tok, D), F32),
            jax.ShapeDtypeStruct((tok, D), F32),
            jax.ShapeDtypeStruct((n * shard, D), F32),
            jax.ShapeDtypeStruct((n * shard, D), F32),
        ],
        scratch_shapes=[
            pltpu.VMEM((tok, D), F32),
            pltpu.VMEM((tok, D), F32),
            pltpu.VMEM((n * shard, D), F32),
            pltpu.VMEM((n * shard, D), F32),
            pltpu.VMEM(dkv.shape, F32),
            pltpu.VMEM(backk.shape, BF16),
            pltpu.VMEM(backv.shape, BF16),
            pltpu.VMEM(glob.shape, BF16),
            pltpu.VMEM((tok, D), F32),
            pltpu.VMEM((tok, D), F32),
            pltpu.VMEM((tok, HEADS * D), F32),
            pltpu.SemaphoreType.DMA((8,)),
            pltpu.SemaphoreType.DMA((8,)),
            pltpu.SemaphoreType.DMA((10,)),
        ],
        compiler_params=pltpu.CompilerParams(vmem_limit_bytes=60 << 20),
        name="final",
    )(index, dq, dkv, backk, backv, glob, c, s)


def on_device(queries, keys, values, dout, glob_keys, glob_values, frames, far_owner, far_local):
    n = lax.axis_size("ctx")
    dq, dkv, backk, backv, glob, c, s, index = main(
        far_owner.T, far_local.T, frames.reshape(-1, LANES), jnp.asarray(frequencies()),
        keys, values.reshape(-1, BLOCK, D), glob_keys, glob_values, queries, dout, n,
    )
    return tuple(final(index, dq, dkv, backk, backv, glob, c, s))


def solution(mesh):
    both = P(("grp", "ctx"), None)
    one = P("grp", None)
    return jax.shard_map(
        on_device,
        mesh=mesh,
        in_specs=(both, both, both, both, one, one, P(("grp", "ctx")), one, one),
        out_specs=(both, both, both, one, one),
        check_vma=False,
    )
```

```python
import functools
import math

import jax
import jax.numpy as jnp
import numpy as np
from jax import lax
from jax.experimental import pallas as pl
from jax.experimental.pallas import tpu as pltpu
from jax.sharding import PartitionSpec as P

F32, BF16 = jnp.float32, jnp.bfloat16
MESH = pl.DeviceIdType.MESH
BLOCK, FAR, SLOTS, D, HEADS = 64, 2, 2, 128, 8
ROWS = BLOCK * HEADS

rope_base = 1000000.0
yarn_factor = 4.0
orig_context = 32768.0
ramp_low = 1.0
ramp_high = 32.0

FACTOR = (0.1 * math.log(yarn_factor) + 1.0) ** 2 / math.sqrt(D)
FACTOR2 = FACTOR * math.log2(math.e)

LANES = 128

NT = (((1,), (1,)), ((), ()))
NN = (((1,), (0,)), ((), ()))
TN = (((0,), (0,)), ((), ()))


def dot(a, b, dims):
    return lax.dot_general(a, b, dims, preferred_element_type=F32)


def frequencies():
    index = np.arange(D // 2, dtype=np.float64)
    inverse = rope_base ** (-2.0 * index / D)
    ratios = orig_context * inverse / (2.0 * math.pi)
    ramp = np.clip((ratios - ramp_low) / (ramp_high - ramp_low), 0.0, 1.0)
    frequency = inverse * ((1.0 - ramp) / yarn_factor + ramp)
    return np.concatenate([frequency, frequency])[None, :].astype(np.float32)


def rot(x, c, s):
    return x * c + pltpu.roll(x, D // 2, 1) * s


def unrot(x, c, s):
    return x * c - pltpu.roll(x, D // 2, 1) * s


def send_plan(i, n):
    return 1 + lax.rem(i * 12, n - 1)


def main_kernel(
    n, owner_ref, place_ref, frame_ref, freq_ref, k_hbm, v_hbm, gk_hbm, gv_hbm, q_hbm, do_hbm,
    dq_hbm, dkv_hbm, backk_ref, backv_ref, glob_ref, c_hbm, s_hbm, index_ref,
    c_ref, s_ref, k_ref,
    ownk, ownv, sendk, sendv, recvk, recvv, retk, retv, rsendk, rsendv,
    kset, vset, qin, din, qr, dor, dsb, pb, pfar, dqs, dkvs, stats, gacc, part, parts, gsum,
    entry, slot,
    qsem, dsem, osem, kfs, kfr, vfs, vfr, kbs, kbr, vbs, vbr, rs, rr, gs, gr, lsem,
):
    me = lax.axis_index("ctx")
    blocks = ownk.shape[0]
    g = gk_hbm.shape[0]
    near = g + BLOCK
    shard = g // n
    barrier = pltpu.get_barrier_semaphore()

    def peer(i):
        return lax.rem(me + send_plan(i, n), n)

    def over(f, count=n - 1, start=0):
        def body(i, carry):
            f(i)
            return carry

        lax.fori_loop(start, count, body, 0)

    over(
        lambda i: pl.semaphore_signal(
            barrier, inc=1, device_id={"ctx": peer(i)}, device_id_type=MESH
        )
    )

    def rows(b):
        return pl.ds(pl.multiple_of(b * BLOCK, BLOCK), BLOCK)

    def qcopy(b):
        return pltpu.make_async_copy(q_hbm.at[rows(b)], qin.at[b], qsem.at[b])

    def dcopy(b):
        return pltpu.make_async_copy(do_hbm.at[rows(b)], din.at[b], dsem.at[b])

    def ocopy(b):
        return pltpu.make_async_copy(dqs.at[b], dq_hbm.at[rows(b)], osem.at[b])

    def fetch(b):
        qcopy(b).start()
        dcopy(b).start()

    brought = [
        pltpu.make_async_copy(src, dst, lsem.at[6 + i])
        for i, (src, dst) in enumerate(
            [(k_hbm, k_ref), (v_hbm, ownv),
             (gk_hbm, kset.at[pl.ds(0, g)]), (gv_hbm, vset.at[pl.ds(0, g)])]
        )
    ]
    for x in brought:
        x.start()
    over(fetch, blocks)

    half = blocks * BLOCK // 2
    low = lax.broadcasted_iota(jnp.int32, (LANES, LANES), 1) < D // 2
    for i in range(half // LANES):
        spread = [
            jnp.broadcast_to(frame_ref[j : j + 1].astype(F32), (LANES, LANES)).T
            for j in (i, i + half // LANES)
        ]
        angle = jnp.where(low, spread[0], spread[1]) * freq_ref[...]
        cosine, sine = jnp.cos(angle), jnp.sin(angle)
        cturn, sturn = pltpu.roll(cosine, D // 2, 1), pltpu.roll(sine, D // 2, 1)
        r0 = slice(i * LANES, (i + 1) * LANES)
        r1 = slice(half + i * LANES, half + (i + 1) * LANES)
        c_ref[r0] = jnp.where(low, cosine, cturn)
        s_ref[r0] = jnp.where(low, -sine, sturn)
        c_ref[r1] = jnp.where(low, cturn, cosine)
        s_ref[r1] = jnp.where(low, -sturn, sine)
    tables = [
        pltpu.make_async_copy(c_ref, c_hbm, lsem.at[4]),
        pltpu.make_async_copy(s_ref, s_hbm, lsem.at[5]),
    ]
    for t in tables:
        t.start()

    def turn(b):
        x = k_ref[rows(b)].astype(F32)
        ownk[b] = rot(x, c_ref[rows(b)], s_ref[rows(b)]).astype(BF16)

    brought[0].wait()
    over(turn, blocks)

    def find(row, wanted, value):
        first = second = jnp.int32(-1)
        for b in reversed(range(blocks)):
            for f in reversed(range(FAR)):
                hit = owner_ref[f, row * blocks + b] == wanted
                second = jnp.where(hit, first, second)
                first = jnp.where(hit, value(f, b), first)
        return first, second

    def listed(d):
        for j, x in enumerate(find(d, me, lambda f, b: place_ref[f, d * blocks + b])):
            index_ref[d * SLOTS + j] = x

    def pair(ref, i):
        return ref.at[pl.ds(pl.multiple_of(i * SLOTS, SLOTS), SLOTS)]

    def remote(src, dst, ssem, rsem, i):
        return pltpu.make_async_remote_copy(
            src, dst, ssem.at[i], rsem.at[i], device_id={"ctx": peer(i)}, device_id_type=MESH
        )

    def kcopy(i):
        return remote(pair(sendk, peer(i)), pair(recvk, me), kfs, kfr, i)

    def vcopy(i):
        return remote(pair(sendv, peer(i)), pair(recvv, me), vfs, vfr, i)

    def kback(i):
        return remote(pair(rsendk, peer(i)), pair(backk_ref, me), kbs, kbr, i)

    def vback(i):
        return remote(pair(rsendv, peer(i)), pair(backv_ref, me), vbs, vbr, i)

    def rcopy(i):
        return remote(part.at[peer(i)], parts.at[me], rs, rr, i)

    def gcopy(i):
        return remote(gsum, glob_ref.at[me], gs, gr, i)

    def lay(dst, src, to, table):
        for j in range(SLOTS):
            dst[to * SLOTS + j] = src[jnp.maximum(table[to * SLOTS + j], 0)]

    pl.semaphore_wait(barrier, n - 1)

    def give_k(i):
        listed(peer(i))
        lay(sendk, ownk, peer(i), index_ref)
        kcopy(i).start()

    def give_v(i):
        lay(sendv, ownv, peer(i), index_ref)
        vcopy(i).start()

    over(give_k)
    brought[1].wait()
    over(give_v)
    listed(me)
    lay(recvk, ownk, me, index_ref)
    lay(recvv, ownv, me, index_ref)

    def mine(o):
        for j, x in enumerate(find(me, o, lambda f, b: jnp.int32(b * FAR + f))):
            entry[o * SLOTS + j] = x

    over(mine, n)

    def seat(b):
        for f in range(FAR):
            o = owner_ref[f, me * blocks + b]
            later = entry[o * SLOTS] != b * FAR + f
            slot[b * FAR + f] = o * SLOTS + later.astype(jnp.int32)

    over(seat, blocks)

    brought[2].wait()
    brought[3].wait()
    width = 512

    def near_stats(b):
        qcopy(b).wait()
        dcopy(b).wait()
        kset[g:near] = ownk[b]
        vset[g:near] = ownv[b]
        c, s = c_ref[rows(b)], s_ref[rows(b)]
        for h in range(HEADS):
            at, cols = slice(h * BLOCK, (h + 1) * BLOCK), slice(h * D, (h + 1) * D)
            qr[b, at] = rot(qin[b, :, cols].astype(F32), c, s).astype(BF16)
            dor[b, at] = din[b, :, cols]
        for j in range(0, ROWS, width):
            at = slice(j, j + width)
            scores = dot(kset[:near], qr[b, at], NT)
            dp = dot(vset[:near], dor[b, at], NT)
            top = jnp.max(scores, axis=0, keepdims=True)
            e = jnp.exp2(scores * FACTOR2 - top * FACTOR2)
            stats[b, 0:1, at] = top
            stats[b, 1:2, at] = jnp.sum(e, axis=0, keepdims=True)
            stats[b, 2:3, at] = jnp.sum(e * dp, axis=0, keepdims=True)

    over(near_stats, blocks)

    over(lambda i: kcopy(i).wait_recv())

    def halves(x):
        return [x[f * BLOCK : (f + 1) * BLOCK] for f in range(FAR)]

    def far_values(b):
        fk = jnp.concatenate([recvk[slot[b * FAR + f]] for f in range(FAR)], axis=0)
        scores = dot(fk, qr[b], NT)
        top0 = stats[b, 0:1, :]
        top = jnp.maximum(jnp.max(scores, axis=0, keepdims=True), top0)
        shrink = jnp.exp2(top0 * FACTOR2 - top * FACTOR2)
        e = jnp.exp2(scores * FACTOR2 - top * FACTOR2)
        total = stats[b, 1:2, :] * shrink + jnp.sum(e, axis=0, keepdims=True)
        w = 1.0 / total
        p = e * w
        pfar[b] = p
        stats[b, 3:4, :] = top * FACTOR2 + jnp.log(total) * math.log2(math.e)
        stats[b, 4:5, :] = stats[b, 2:3, :] * shrink * w
        for f, x in enumerate(halves(dot(p.astype(BF16), dor[b], NN))):
            retv[b * FAR + f] = x.astype(BF16)

    over(far_values, blocks)

    def return_v(i):
        lay(rsendv, retv, peer(i), entry)
        vback(i).start()

    over(return_v)

    over(lambda i: vcopy(i).wait_recv())

    def far_keys(b):
        fv = jnp.concatenate([recvv[slot[b * FAR + f]] for f in range(FAR)], axis=0)
        dp = dot(fv, dor[b], NT)
        p = pfar[b]
        delta = stats[b, 4:5, :] + jnp.sum(p * dp, axis=0, keepdims=True)
        stats[b, 5:6, :] = delta
        ds = (p * (dp - delta)).astype(BF16)
        dsb[b, near:] = ds
        for f, x in enumerate(halves(dot(ds, qr[b], NN) * FACTOR)):
            retk[b * FAR + f] = x.astype(BF16)

    over(far_keys, blocks)

    def return_k(i):
        lay(rsendk, retk, peer(i), entry)
        kback(i).start()

    over(return_k, 24)
    lay(rsendk, retk, me, entry)
    lay(rsendv, retv, me, entry)
    keptk = pltpu.make_async_copy(pair(rsendk, me), pair(backk_ref, me), lsem.at[0])
    keptv = pltpu.make_async_copy(pair(rsendv, me), pair(backv_ref, me), lsem.at[1])
    keptk.start()
    keptv.start()

    gacc[...] = jnp.zeros_like(gacc)

    def near_pass(b):
        kset[g:near] = ownk[b]
        vset[g:near] = ownv[b]
        for j in range(0, ROWS, width):
            at = slice(j, j + width)
            scores = dot(kset[:near], qr[b, at], NT)
            dp = dot(vset[:near], dor[b, at], NT)
            p = jnp.exp2(scores * FACTOR2 - stats[b, 3:4, at])
            pb[:, at] = p.astype(BF16)
            dsb[b, :near, at] = (p * (dp - stats[b, 5:6, at])).astype(BF16)
        dk = dot(dsb[b, :near], qr[b], NN) * FACTOR
        dv = dot(pb[...], dor[b], NN)
        gacc[:, :D] += dk[:g]
        gacc[:, D:] += dv[:g]
        dkvs[b, :, :D] = dk[g:]
        dkvs[b, :, D:] = dv[g:]

    over(near_pass, blocks)
    for i in range(n):
        part[i] = gacc[i * shard : (i + 1) * shard].astype(BF16)
    over(lambda i: rcopy(i).start())
    over(return_k, n - 1, 24)
    parts[me] = part[me]
    owned = pltpu.make_async_copy(dkvs, dkv_hbm, lsem.at[2])
    owned.start()

    def query_pass(b):
        kset[g:near] = ownk[b]
        for f in range(FAR):
            kset[near + f * BLOCK : near + (f + 1) * BLOCK] = recvk[slot[b * FAR + f]]
        dq = dot(dsb[b], kset[...], TN) * FACTOR
        c, s = c_ref[rows(b)], s_ref[rows(b)]
        for h in range(HEADS):
            dqs[b, :, h * D : (h + 1) * D] = unrot(dq[h * BLOCK : (h + 1) * BLOCK], c, s)
        ocopy(b).start()

    over(query_pass, 10)

    over(lambda i: rcopy(i).wait_recv())
    gsum[...] = jnp.sum(parts[...].astype(F32), axis=0).astype(BF16)
    over(lambda i: gcopy(i).start())
    kept = pltpu.make_async_copy(gsum, glob_ref.at[me], lsem.at[3])
    kept.start()
    over(query_pass, blocks, 10)
    over(lambda i: kcopy(i).wait_send())
    over(lambda i: vcopy(i).wait_send())
    over(lambda i: rcopy(i).wait_send())
    over(lambda b: ocopy(b).wait(), blocks)
    for t in tables:
        t.wait()
    owned.wait()
    keptk.wait()
    keptv.wait()
    kept.wait()
    over(lambda i: vback(i).wait())
    over(lambda i: kback(i).wait())
    over(lambda i: gcopy(i).wait())


def main(owner, place, frames, freq, keys, values, gk, gv, q, do, n):
    tok = keys.shape[0]
    blocks = tok // BLOCK
    g = gk.shape[0]
    shard = g // n
    near = g + BLOCK
    smem, vmem, any_ = (pl.BlockSpec(memory_space=m) for m in (pltpu.SMEM, pltpu.VMEM, pl.ANY))
    dma = lambda k: pltpu.SemaphoreType.DMA((k,))
    slots = pltpu.VMEM((n * SLOTS, BLOCK, D), BF16)
    mine = pltpu.VMEM((blocks, BLOCK, D), BF16)
    ends = pltpu.VMEM((blocks * FAR, BLOCK, D), BF16)
    return pl.pallas_call(
        functools.partial(main_kernel, n),
        in_specs=[smem] * 2 + [vmem] * 2 + [any_] * 6,
        out_specs=[any_] * 7 + [smem],
        out_shape=[
            jax.ShapeDtypeStruct((tok, HEADS * D), F32),
            jax.ShapeDtypeStruct((blocks, BLOCK, 2 * D), F32),
            jax.ShapeDtypeStruct((n * SLOTS, BLOCK, D), BF16),
            jax.ShapeDtypeStruct((n * SLOTS, BLOCK, D), BF16),
            jax.ShapeDtypeStruct((n, shard, 2 * D), BF16),
            jax.ShapeDtypeStruct((tok, D), F32),
            jax.ShapeDtypeStruct((tok, D), F32),
            jax.ShapeDtypeStruct((n * SLOTS,), jnp.int32),
        ],
        scratch_shapes=[
            pltpu.VMEM((tok, D), F32),
            pltpu.VMEM((tok, D), F32),
            pltpu.VMEM((tok, D), BF16),
            mine, mine, slots, slots, slots, slots, ends, ends, slots, slots,
            pltpu.VMEM((near + FAR * BLOCK, D), BF16),
            pltpu.VMEM((near, D), BF16),
            pltpu.VMEM((blocks, BLOCK, HEADS * D), BF16),
            pltpu.VMEM((blocks, BLOCK, HEADS * D), BF16),
            pltpu.VMEM((blocks, ROWS, D), BF16),
            pltpu.VMEM((blocks, ROWS, D), BF16),
            pltpu.VMEM((blocks, near + FAR * BLOCK, ROWS), BF16),
            pltpu.VMEM((near, ROWS), BF16),
            pltpu.VMEM((blocks, FAR * BLOCK, ROWS), F32),
            pltpu.VMEM((blocks, BLOCK, HEADS * D), F32),
            pltpu.VMEM((blocks, BLOCK, 2 * D), F32),
            pltpu.VMEM((blocks, 8, ROWS), F32),
            pltpu.VMEM((g, 2 * D), F32),
            pltpu.VMEM((n, shard, 2 * D), BF16),
            pltpu.VMEM((n, shard, 2 * D), BF16),
            pltpu.VMEM((shard, 2 * D), BF16),
            pltpu.SMEM((n * SLOTS,), jnp.int32),
            pltpu.SMEM((blocks * FAR,), jnp.int32),
            dma(blocks), dma(blocks), dma(blocks),
        ] + [dma(n)] * 12 + [dma(10)],
        compiler_params=pltpu.CompilerParams(
            collective_id=0, has_side_effects=True, vmem_limit_bytes=58 << 20
        ),
        name="main",
    )(owner, place, frames, freq, keys, values, gk, gv, q, do)


def final_kernel(
    index_ref, dq_hbm, dkv_hbm, backk_hbm, backv_hbm, glob_hbm, c_hbm, s_hbm,
    qg_hbm, kg_hbm, vg_hbm, gk_hbm, gv_hbm,
    kg_ref, vg_ref, gk_ref, gv_ref, acc, backk, backv, glob, c, s, held, isem, osem, sem,
):
    blocks = acc.shape[0]
    n, shard, _ = glob.shape
    total = backk.shape[0]
    tok = blocks * BLOCK
    pieces = isem.shape[0]
    step = tok // pieces
    loads = [
        pltpu.make_async_copy(src, dst, sem.at[i])
        for i, (src, dst) in enumerate(
            [(dkv_hbm, acc), (backk_hbm, backk), (backv_hbm, backv),
             (c_hbm, c), (s_hbm, s), (glob_hbm, glob)]
        )
    ]
    parts = [pl.ds(i * step, step) for i in range(pieces)]
    ins = [pltpu.make_async_copy(dq_hbm.at[r], held.at[r], isem.at[i]) for i, r in enumerate(parts)]
    outs = [pltpu.make_async_copy(held.at[r], qg_hbm.at[r], osem.at[i]) for i, r in enumerate(parts)]
    for m in loads + ins:
        m.start()
    stores = [
        pltpu.make_async_copy(src, dst, sem.at[6 + i])
        for i, (src, dst) in enumerate(
            [(gk_ref, gk_hbm), (gv_ref, gv_hbm), (kg_ref, kg_hbm), (vg_ref, vg_hbm)]
        )
    ]
    for m in loads[:3]:
        m.wait()

    def add(i, carry):
        at = index_ref[i]

        @pl.when(at >= 0)
        def _():
            acc[at, :, :D] += backk[i].astype(F32)
            acc[at, :, D:] += backv[i].astype(F32)

        return carry

    lax.fori_loop(0, total // 2, add, 0, unroll=4)
    for i, m in enumerate(ins):
        m.wait()
        outs[i].start()
    lax.fori_loop(total // 2, total, add, 0, unroll=4)
    for m in loads[3:]:
        m.wait()
    for b in range(blocks):
        r = slice(b * BLOCK, (b + 1) * BLOCK)
        kg_ref[r] = unrot(acc[b, :, :D], c[r], s[r])
        vg_ref[r] = acc[b, :, D:]
    stores[2].start()
    stores[3].start()
    for i in range(n):
        gk_ref[i * shard : (i + 1) * shard] = glob[i, :, :D].astype(F32)
        gv_ref[i * shard : (i + 1) * shard] = glob[i, :, D:].astype(F32)
    stores[0].start()
    stores[1].start()
    for m in outs + stores:
        m.wait()


def final(index, dq, dkv, backk, backv, glob, c, s):
    blocks = dkv.shape[0]
    tok = blocks * BLOCK
    n, shard, _ = glob.shape
    smem, vmem, any_ = (pl.BlockSpec(memory_space=m) for m in (pltpu.SMEM, pltpu.VMEM, pl.ANY))
    return pl.pallas_call(
        final_kernel,
        in_specs=[smem] + [any_] * 7,
        out_specs=[any_] * 5,
        out_shape=[
            jax.ShapeDtypeStruct((tok, HEADS * D), F32),
            jax.ShapeDtypeStruct((tok, D), F32),
            jax.ShapeDtypeStruct((tok, D), F32),
            jax.ShapeDtypeStruct((n * shard, D), F32),
            jax.ShapeDtypeStruct((n * shard, D), F32),
        ],
        scratch_shapes=[
            pltpu.VMEM((tok, D), F32),
            pltpu.VMEM((tok, D), F32),
            pltpu.VMEM((n * shard, D), F32),
            pltpu.VMEM((n * shard, D), F32),
            pltpu.VMEM(dkv.shape, F32),
            pltpu.VMEM(backk.shape, BF16),
            pltpu.VMEM(backv.shape, BF16),
            pltpu.VMEM(glob.shape, BF16),
            pltpu.VMEM((tok, D), F32),
            pltpu.VMEM((tok, D), F32),
            pltpu.VMEM((tok, HEADS * D), F32),
            pltpu.SemaphoreType.DMA((8,)),
            pltpu.SemaphoreType.DMA((8,)),
            pltpu.SemaphoreType.DMA((10,)),
        ],
        compiler_params=pltpu.CompilerParams(vmem_limit_bytes=60 << 20),
        name="final",
    )(index, dq, dkv, backk, backv, glob, c, s)


def on_device(queries, keys, values, dout, glob_keys, glob_values, frames, far_owner, far_local):
    n = lax.axis_size("ctx")
    dq, dkv, backk, backv, glob, c, s, index = main(
        far_owner.T, far_local.T, frames.reshape(-1, LANES), jnp.asarray(frequencies()),
        keys, values.reshape(-1, BLOCK, D), glob_keys, glob_values, queries, dout, n,
    )
    return tuple(final(index, dq, dkv, backk, backv, glob, c, s))


def solution(mesh):
    both = P(("grp", "ctx"), None)
    one = P("grp", None)
    return jax.shard_map(
        on_device,
        mesh=mesh,
        in_specs=(both, both, both, both, one, one, P(("grp", "ctx")), one, one),
        out_specs=(both, both, both, one, one),
        check_vma=False,
    )
```
